32 devices in a mesh: seq: 8 (over y, x, core), head: 4 (over z).
Axes of the slice: x: 2, y: 2, z: 4, core: 2. Of those that a mesh axis runs over, the one named last changes fastest.
Arguments:
- patch_embed: bfloat16 [4, 1024, 1280], P('head', 'seq'), may hold values from -6 to 6
- perturbation: float32 [4, 1024, 1280], P('head', 'seq'), may hold values from -3 to 3
- target: bfloat16 [4, 1024, 1280], P('head', 'seq'), may hold values from -6 to 6
- ln_gain: float32 [1280], replicated, may hold values from 0.5 to 1.5
- ln_bias: float32 [1280], replicated, may hold values from -1.5 to 1.5
- w_qkv: bfloat16 [16, 240, 1280], P('head'), may hold values from -10.0623059 to 10.0623059
- w_out: bfloat16 [16, 80, 1280], P('head'), may hold values from -0.15625 to 0.15625
- radius: float32 [4], replicated, may hold values from 137.38402 to 423.6007
- step_size: float32 [4], replicated, may hold values from 34.346004 to 137.38402
Outputs:
- perturbation_out: float32 [4, 1024, 1280], P('head', 'seq')
The draws below stay inside these ranges and needn't reach their ends.
All inputs are finite; a program needn't handle non-finite values.
Results may differ from the reference program's by a relative error of at most 0.001.
Values may be sent and summed in bfloat16 or wider, within the bound.
No kernel may reach another device: no remote copies, remote signals or barrier semaphores. Data moves between devices by JAX's collectives and lax.ppermute only.
A program may use at most 64 MiB of HBM per device.

```python
import math
import jax
import jax.numpy as jnp
from jax import lax

D = 1280
HEADS = 16
HD = 80
PATCHES = 1024
PGD_STEPS = 1
EXAMPLES = 4


def draw_w_qkv(key, part):
    entries = jax.random.truncated_normal(key, -6.0, 6.0, (HEADS, 3 * HD, D), jnp.float32) / math.sqrt(D)
    return entries.astype(jnp.bfloat16)


def levels(stream_key, dims, shards, smallest, top_value):
    def one(position, parts):
        steps = jax.random.uniform(jax.random.fold_in(jax.random.fold_in(stream_key, 6), position), (parts,), jnp.float32, smallest / len(shards), top_value / len(shards))
        return jnp.repeat(jnp.exp(steps), dims[position] // parts).reshape((-1,) + (1,) * (len(dims) - position - 1))

    gain = one(*shards[0])
    for cut in shards[1:]:
        gain = gain * one(*cut)
    return gain


def gaussian(own_key, extent, scale, limit, shards=(), held_as=jnp.bfloat16):
    values = scale * jax.random.normal(own_key, extent, jnp.float32)
    if shards:
        values = values * levels(own_key, extent, shards, -0.22, 0.18)
    return jnp.clip(values, -limit, limit).astype(held_as)


def setup_inputs(seed: int = 0) -> dict:
    splits = jax.random.split(jax.random.key(seed), 10)
    return {
        "patch_embed": gaussian(splits[0], (EXAMPLES, PATCHES, D), 1.0, 6.0, ((0, 4), (1, 8))),
        "perturbation": gaussian(splits[1], (EXAMPLES, PATCHES, D), 0.5, 3.0, ((0, 4), (1, 8)), jnp.float32),
        "target": gaussian(splits[2], (EXAMPLES, PATCHES, D), 1.0, 6.0, ((0, 4), (1, 8))),
        "ln_gain": jnp.clip(1.0 + 0.1 * jax.random.normal(splits[3], (D,), jnp.float32), 0.5, 1.5),
        "ln_bias": gaussian(splits[4], (D,), 0.3, 1.5, (), jnp.float32),
        "w_qkv": draw_w_qkv(jax.random.fold_in(splits[9], 71), 0),
        "w_out": gaussian(splits[6], (HEADS, HD, D), (HEADS * HD) ** -0.5, 0.15625, ((0, 4),)),
        "radius": jnp.clip(jnp.exp(jax.random.uniform(splits[7], (EXAMPLES,), jnp.float32, math.log(137.38402), math.log(423.6007))), 137.38402, 423.6007),
        "step_size": jnp.clip(jnp.exp(jax.random.uniform(splits[8], (EXAMPLES,), jnp.float32, math.log(34.346004), math.log(137.38402))), 34.346004, 137.38402),
    }


norm_epsilon = 1e-06
layer_epsilon = 1e-06

def layer_statistics(gathered):
    center = gathered - lax.optimization_barrier(jnp.mean(gathered, axis=-1, keepdims=True))
    variance = lax.optimization_barrier(jnp.mean(center * center, axis=-1, keepdims=True))
    inverse = lax.rsqrt(variance + layer_epsilon)
    return (center * inverse, inverse)

def forward_pair(packed):
    score_scale = 1.0 / math.sqrt(HD)
    queries = packed[:, :HD]
    key_rows = packed[:, HD:2 * HD]
    values = packed[:, 2 * HD:]
    scores = jnp.dot(queries, key_rows.T, preferred_element_type=jnp.float32) * score_scale
    row_max = lax.optimization_barrier(jnp.max(scores, axis=-1, keepdims=True))
    log_total = row_max + jnp.log(lax.optimization_barrier(jnp.sum(jnp.exp(scores - row_max), axis=-1, keepdims=True)))
    weights = jnp.exp(scores - log_total).astype(jnp.bfloat16)
    output = jnp.dot(weights, values, preferred_element_type=jnp.float32).astype(jnp.bfloat16)
    return (output, log_total[:, 0])

def backward_pair(inputs):
    packed, output, log_total, grad_output = inputs
    score_scale = 1.0 / math.sqrt(HD)
    queries = packed[:, :HD]
    key_rows = packed[:, HD:2 * HD]
    values = packed[:, 2 * HD:]
    scores = jnp.dot(queries, key_rows.T, preferred_element_type=jnp.float32) * score_scale
    weights = jnp.exp(scores - log_total[:, None])
    row_dot = lax.optimization_barrier(jnp.sum(grad_output.astype(jnp.float32) * output.astype(jnp.float32), axis=-1))
    grad_values = jnp.dot(weights.astype(jnp.bfloat16).T, grad_output, preferred_element_type=jnp.float32)
    grad_weights = jnp.dot(grad_output, values.T, preferred_element_type=jnp.float32)
    grad_scores = (weights * (grad_weights - row_dot[:, None]) * score_scale).astype(jnp.bfloat16)
    grad_query = jnp.dot(grad_scores, key_rows, preferred_element_type=jnp.float32)
    grad_keys = jnp.dot(grad_scores.T, queries, preferred_element_type=jnp.float32)
    return jnp.concatenate([grad_query.astype(jnp.bfloat16), grad_keys.astype(jnp.bfloat16), grad_values.astype(jnp.bfloat16)], axis=-1)

def reference(patch_embed, perturbation, target, ln_gain, ln_bias, w_qkv, w_out, radius, step_size):
    highest = lax.Precision.HIGHEST
    weights_in = w_qkv.astype(jnp.float32)
    weights_back = w_out.astype(jnp.float32)
    current = perturbation
    for attempt in range(PGD_STEPS):
        mixed = patch_embed.astype(jnp.float32) + current
        rounded = lax.optimization_barrier(mixed.astype(jnp.bfloat16))
        normed, inverse = layer_statistics(rounded.astype(jnp.float32))
        hidden = (normed * ln_gain + ln_bias).astype(jnp.bfloat16)
        packed = jnp.einsum('epd,hcd->ehpc', hidden.astype(jnp.float32), weights_in, precision=highest).astype(jnp.bfloat16)
        pair_rows = packed.reshape(EXAMPLES * HEADS, PATCHES, 3 * HD)
        output, log_total = lax.map(forward_pair, pair_rows)
        output_heads = output.reshape(EXAMPLES, HEADS, PATCHES, HD)
        branch = jnp.einsum('ehpc,hcd->epd', output_heads.astype(jnp.float32), weights_back, precision=highest)
        result = mixed + branch
        residual = result - target.astype(jnp.float32)
        residual_half = residual.astype(jnp.bfloat16)
        grad_output = jnp.einsum('epd,hcd->ehpc', residual_half.astype(jnp.float32), weights_back, precision=highest).astype(jnp.bfloat16)
        grad_packed = lax.map(backward_pair, (pair_rows, output, log_total, grad_output.reshape(EXAMPLES * HEADS, PATCHES, HD)))
        grad_packed = grad_packed.reshape(EXAMPLES, HEADS, PATCHES, 3 * HD)
        grad_hidden = jnp.einsum('ehpc,hcd->epd', grad_packed.astype(jnp.float32), weights_in, precision=highest)
        scaled = grad_hidden * ln_gain
        first_mean = lax.optimization_barrier(jnp.mean(scaled, axis=-1, keepdims=True))
        second_mean = lax.optimization_barrier(jnp.mean(scaled * normed, axis=-1, keepdims=True))
        grad_input = (scaled - first_mean - normed * second_mean) * inverse
        gradient = residual + grad_input
        grad_square = lax.optimization_barrier(jnp.sum(gradient * gradient, axis=(1, 2)))
        stepped = current + (step_size / jnp.sqrt(grad_square + norm_epsilon))[:, None, None] * gradient
        stepped_square = lax.optimization_barrier(jnp.sum(stepped * stepped, axis=(1, 2)))
        current = stepped * jnp.minimum(1.0, radius / jnp.sqrt(stepped_square + norm_epsilon))[:, None, None]
    return current
```

```python
import functools
import math

import jax
import jax.numpy as jnp
from jax import lax
from jax.experimental import pallas as pl
from jax.experimental.pallas import tpu as pltpu
from jax.sharding import PartitionSpec as P

norm_epsilon = 1e-06
layer_epsilon = 1e-06


def layer_statistics(gathered):
    center = gathered - jnp.mean(gathered, axis=-1, keepdims=True)
    variance = jnp.mean(center * center, axis=-1, keepdims=True)
    inverse = lax.rsqrt(variance + layer_epsilon)
    return (center * inverse, inverse)


def attend_forward(queries, key_rows, values, score_scale):
    item_count, length, head_dim = queries.shape
    block_rows = min(512, length)
    query_blocks = queries.reshape(item_count, length // block_rows, block_rows, head_dim).swapaxes(
        0, 1
    )

    def one_block(query_block):
        scores = (
            jnp.einsum("nqe,nke->nqk", query_block, key_rows, preferred_element_type=jnp.float32)
            * score_scale
        )
        row_max = jnp.max(scores, axis=-1, keepdims=True)
        log_total = row_max + jnp.log(jnp.sum(jnp.exp(scores - row_max), axis=-1, keepdims=True))
        weights = jnp.exp(scores - log_total).astype(jnp.bfloat16)
        output = jnp.einsum(
            "nqk,nke->nqe", weights, values, preferred_element_type=jnp.float32
        ).astype(jnp.bfloat16)
        return (output, log_total[..., 0])

    output, log_total = lax.map(one_block, query_blocks)
    output = output.swapaxes(0, 1).reshape(item_count, length, head_dim)
    log_total = log_total.swapaxes(0, 1).reshape(item_count, length)
    return (output, log_total)


def attend_backward(queries, key_rows, values, output, log_total, grad_output, score_scale):
    item_count, length, head_dim = queries.shape
    block_rows = min(512, length)
    block_count = length // block_rows

    def cut_rows(array):
        return array.reshape((item_count, block_count, block_rows) + array.shape[2:]).swapaxes(0, 1)

    row_dot = jnp.sum(grad_output.astype(jnp.float32) * output.astype(jnp.float32), axis=-1)

    def one_block(carry, inputs):
        grad_keys, grad_values = carry
        query_block, grad_block, total_block, dot_block = inputs
        scores = (
            jnp.einsum("nqe,nke->nqk", query_block, key_rows, preferred_element_type=jnp.float32)
            * score_scale
        )
        weights = jnp.exp(scores - total_block[..., None])
        grad_values = grad_values + jnp.einsum(
            "nqk,nqe->nke",
            weights.astype(jnp.bfloat16),
            grad_block,
            preferred_element_type=jnp.float32,
        )
        grad_weights = jnp.einsum(
            "nqe,nke->nqk", grad_block, values, preferred_element_type=jnp.float32
        )
        grad_scores = (weights * (grad_weights - dot_block[..., None]) * score_scale).astype(
            jnp.bfloat16
        )
        grad_query = jnp.einsum(
            "nqk,nke->nqe", grad_scores, key_rows, preferred_element_type=jnp.float32
        ).astype(jnp.bfloat16)
        grad_keys = grad_keys + jnp.einsum(
            "nqk,nqe->nke", grad_scores, query_block, preferred_element_type=jnp.float32
        )
        return ((grad_keys, grad_values), grad_query)

    zero_rows = jnp.zeros((item_count, length, head_dim), jnp.float32)
    (grad_keys, grad_values), grad_query = lax.scan(
        one_block,
        (zero_rows, zero_rows),
        (cut_rows(queries), cut_rows(grad_output), cut_rows(log_total), cut_rows(row_dot)),
    )
    grad_query = grad_query.swapaxes(0, 1).reshape(item_count, length, head_dim)
    return jnp.concatenate(
        [grad_query, grad_keys.astype(jnp.bfloat16), grad_values.astype(jnp.bfloat16)], axis=-1
    )


def general_plan(patch_embed, perturbation, target, ln_gain, ln_bias, w_qkv, w_out, radius, step_size):
    seq_count = lax.axis_size("seq")
    own_images, part_rows, model_width = patch_embed.shape
    local_heads = w_qkv.shape[0]
    head_dim = w_qkv.shape[1] // 3
    examples = own_images * lax.axis_size("head")
    pair_count = examples * local_heads // seq_count
    first_image = lax.axis_index("head") * own_images
    own_step = lax.dynamic_slice_in_dim(step_size, first_image, own_images, 0)
    own_radius = lax.dynamic_slice_in_dim(radius, first_image, own_images, 0)
    score_scale = 1.0 / math.sqrt(head_dim)
    current = perturbation
    mixed = patch_embed.astype(jnp.float32) + current
    rounded = mixed.astype(jnp.bfloat16)
    normed, inverse = layer_statistics(rounded.astype(jnp.float32))
    hidden = (normed * ln_gain + ln_bias).astype(jnp.bfloat16)
    hidden_all = lax.all_gather(hidden, "head", axis=0, tiled=True)
    packed = jnp.einsum(
        "epd,hcd->ehpc", hidden_all, w_qkv, preferred_element_type=jnp.float32
    ).astype(jnp.bfloat16)
    packed = packed.reshape(seq_count, pair_count, part_rows, 3 * head_dim)
    pair_rows = lax.all_to_all(packed, "seq", split_axis=0, concat_axis=2, tiled=True)[0]
    queries = pair_rows[..., :head_dim]
    key_rows = pair_rows[..., head_dim : 2 * head_dim]
    values = pair_rows[..., 2 * head_dim :]
    output, log_total = attend_forward(queries, key_rows, values, score_scale)
    returned = lax.all_to_all(output[None], "seq", split_axis=2, concat_axis=0, tiled=True)
    returned = returned.reshape(examples, local_heads, part_rows, head_dim)
    partial_value = jnp.einsum("ehpc,hcd->epd", returned, w_out, preferred_element_type=jnp.float32)
    branch = lax.psum_scatter(partial_value, "head", scatter_dimension=0, tiled=True)
    result = mixed + branch
    residual = result - target.astype(jnp.float32)
    residual_all = lax.all_gather(residual.astype(jnp.bfloat16), "head", axis=0, tiled=True)
    grad_output = jnp.einsum(
        "epd,hcd->ehpc", residual_all, w_out, preferred_element_type=jnp.float32
    ).astype(jnp.bfloat16)
    grad_output = grad_output.reshape(seq_count, pair_count, part_rows, head_dim)
    grad_pairs = lax.all_to_all(grad_output, "seq", split_axis=0, concat_axis=2, tiled=True)[0]
    grad_packed = attend_backward(
        queries, key_rows, values, output, log_total, grad_pairs, score_scale
    )
    grad_tokens = lax.all_to_all(grad_packed[None], "seq", split_axis=2, concat_axis=0, tiled=True)
    grad_tokens = grad_tokens.reshape(examples, local_heads, part_rows, 3 * head_dim)
    grad_partial = jnp.einsum(
        "ehpc,hcd->epd", grad_tokens, w_qkv, preferred_element_type=jnp.float32
    )
    grad_hidden = lax.psum_scatter(grad_partial, "head", scatter_dimension=0, tiled=True)
    scaled = grad_hidden * ln_gain
    first_mean = jnp.mean(scaled, axis=-1, keepdims=True)
    second_mean = jnp.mean(scaled * normed, axis=-1, keepdims=True)
    grad_input = (scaled - first_mean - normed * second_mean) * inverse
    gradient = residual + grad_input
    grad_square = lax.psum(jnp.sum(gradient * gradient, axis=(1, 2)), "seq")
    stepped = current + (own_step / jnp.sqrt(grad_square + norm_epsilon))[:, None, None] * gradient
    stepped_square = lax.psum(jnp.sum(stepped * stepped, axis=(1, 2)), "seq")
    current = (
        stepped
        * jnp.minimum(1.0, own_radius / jnp.sqrt(stepped_square + norm_epsilon))[:, None, None]
    )
    return current


LOG2E = math.log2(math.e)
bf16 = jnp.bfloat16
f32 = jnp.float32
VMEM = pl.BlockSpec(memory_space=pltpu.VMEM)


def dot(a, b, a_dim, b_dim):
    return lax.dot_general(a, b, (((a_dim,), (b_dim,)), ((), ())), preferred_element_type=f32)


def call(body, outs, *args, flops=0, exps=0, name=None):
    shapes = [jax.ShapeDtypeStruct(shape, dtype) for shape, dtype in outs]
    moved = sum(a.size * a.dtype.itemsize for a in list(args) + shapes)
    return pl.pallas_call(
        body,
        out_shape=shapes,
        in_specs=[VMEM] * len(args),
        out_specs=[VMEM] * len(shapes),
        cost_estimate=pl.CostEstimate(flops=flops, transcendentals=exps, bytes_accessed=moved),
        name=name,
    )(*args)


def norm_parts(embed, current):
    rounded = (embed.astype(f32) + current).astype(bf16).astype(f32)
    center = rounded - jnp.mean(rounded, axis=-1, keepdims=True)
    inverse = lax.rsqrt(jnp.mean(center * center, axis=-1, keepdims=True) + layer_epsilon)
    return center * inverse, inverse


def norm_body(embed, current, gain, bias, hidden):
    normed, _ = norm_parts(embed[...], current[...])
    hidden[...] = (normed * gain[...] + bias[...]).astype(bf16)


def forward_body(chips, *refs):
    weight = refs[0][...]
    hidden = refs[1:-4]
    packed_ref, total_ref, same_ref, other_ref = refs[-4:]
    entries, _ = weight.shape
    head_dim = entries // 3
    rows = same_ref.shape[-1]
    length = packed_ref.shape[1]
    scale = LOG2E / math.sqrt(head_dim)
    parts = [h[...] for h in hidden]
    blocks = []
    for part in parts:
        if blocks and blocks[-1][0] < rows:
            blocks[-1][0] += part.shape[0]
            blocks[-1][1].append(part)
        else:
            blocks.append([part.shape[0], [part]])
    for i in range(0, len(blocks), 2):
        rhs = jnp.concatenate(blocks[i][1] + blocks[i + 1][1], axis=0)
        packed_ref[:, i * rows : (i + 2) * rows] = dot(weight, rhs, 1, 1).astype(bf16)
    keys = packed_ref[head_dim : 2 * head_dim, :].T
    values_t = packed_ref[2 * head_dim :, :]
    step = min(256, length)
    for q in range(0, length, step):
        queries_t = packed_ref[:head_dim, q : q + step]
        scores = dot(keys, queries_t, 1, 0) * scale
        top = jnp.max(scores, axis=0, keepdims=True)
        raised = jnp.exp2(scores - top)
        total = jnp.sum(raised, axis=0, keepdims=True)
        total_ref[:, q : q + step] = top + jnp.log2(total)
        weights = (raised * (1.0 / total)).astype(bf16)
        out = dot(values_t, weights, 1, 0).astype(bf16)
        for r in range(0, step, rows):
            block = (q + r) // rows
            dest = same_ref if block < chips else other_ref
            dest[block % chips] = out[:, r : r + rows]


def project_body(slots, embed, current, target, *refs):
    outs, weights = refs[:slots], refs[slots : 2 * slots]
    same_ref, other_ref, residual_ref = refs[2 * slots :]
    outs_t = jnp.concatenate([o[...] for o in outs], axis=0)
    full = jnp.concatenate([w[...] for w in weights], axis=0)
    branch = dot(outs_t, full, 0, 0)
    residual = embed[...].astype(f32) + current[...] + branch - target[...].astype(f32)
    residual_ref[...] = residual
    grads = dot(full, residual.astype(bf16), 1, 1).astype(bf16)
    chips, heads, head_dim, _ = same_ref.shape
    for head in range(heads):
        for chip in range(chips):
            for core, dest in enumerate((same_ref, other_ref)):
                row = ((head * chips + chip) * 2 + core) * head_dim
                dest[chip, head] = grads[row : row + head_dim, :]


def backward_body(head, chips, packed_ref, total_ref, same_out, other_out, *refs):
    arrived, (same_grad, other_grad) = refs[:chips], refs[chips:]
    entries, length = packed_ref.shape
    head_dim = entries // 3
    scale = 1.0 / math.sqrt(head_dim)
    grads_t = jnp.concatenate(
        [arrived[chip][core, head] for core in range(2) for chip in range(chips)], axis=1
    )
    out_t = jnp.concatenate([ref[chip] for ref in (same_out, other_out) for chip in range(chips)], axis=1)
    queries_t = packed_ref[:head_dim, :]
    keys_t = packed_ref[head_dim : 2 * head_dim, :]
    keys = keys_t.T
    values = packed_ref[2 * head_dim :, :].T
    row_dot = jnp.sum(grads_t.astype(f32) * out_t.astype(f32), axis=0, keepdims=True)
    step = min(256, length)
    grad_keys = jnp.zeros((head_dim, length), f32)
    grad_values = jnp.zeros((head_dim, length), f32)
    half = length // 2
    for q in range(0, length, step):
        cut = slice(q, q + step)
        scores = dot(keys, queries_t[:, cut], 1, 0) * (scale * LOG2E)
        weights = jnp.exp2(scores - total_ref[:, cut])
        grad_weights = dot(values, grads_t[:, cut], 1, 0)
        grad_scores = (weights * (grad_weights - row_dot[:, cut]) * scale).astype(bf16)
        grad_values = grad_values + dot(grads_t[:, cut], weights.astype(bf16), 1, 1)
        grad_keys = grad_keys + dot(queries_t[:, cut], grad_scores, 1, 1)
        grad_query = dot(keys_t, grad_scores, 1, 0).astype(bf16)
        dest = same_grad if q < half else other_grad
        dest[:head_dim, q % half : q % half + step] = grad_query
    for i, dest in enumerate((same_grad, other_grad)):
        dest[head_dim : 2 * head_dim, :] = grad_keys[:, i * half : (i + 1) * half].astype(bf16)
        dest[2 * head_dim :, :] = grad_values[:, i * half : (i + 1) * half].astype(bf16)


def hidden_grad_body(count, *refs):
    grads, weights = refs[:count], refs[count : 2 * count]
    own, sent = refs[2 * count], refs[2 * count + 1 :]
    rows = own.shape[0]
    total = sum(dot(g[...], w[...], 0, 0) for g, w in zip(grads, weights))
    own[...] = total[:rows]
    for i, dest in enumerate(sent):
        dest[...] = total[(i + 1) * rows : (i + 2) * rows].astype(bf16)


def gradient_body(embed, current, residual, gain, own, *refs):
    arrived, (gradient_ref, sums_ref) = refs[:-2], refs[-2:]
    grad_hidden = own[...]
    for part in arrived:
        grad_hidden = grad_hidden + part[...].astype(f32)
    normed, inverse = norm_parts(embed[...], current[...])
    scaled = grad_hidden * gain[...]
    first_mean = jnp.mean(scaled, axis=-1, keepdims=True)
    second_mean = jnp.mean(scaled * normed, axis=-1, keepdims=True)
    gradient = residual[...] + (scaled - first_mean - normed * second_mean) * inverse
    gradient_ref[...] = gradient
    before = current[...]
    lanes = sums_ref.shape[1]
    sums_ref[...] = jnp.zeros_like(sums_ref)
    for i, terms in enumerate((gradient * gradient, before * gradient, before * before)):
        columns = jnp.sum(terms, axis=0, keepdims=True)
        sums_ref[i : i + 1, :] = sum(
            columns[:, j : j + lanes] for j in range(0, columns.shape[1], lanes)
        )


def plane_plan(patch_embed, perturbation, target, ln_gain, ln_bias, w_qkv, w_out, radius, step_size):
    seq_count, planes = lax.axis_size("seq"), lax.axis_size("head")
    place, plane = lax.axis_index("seq"), lax.axis_index("head")
    chips = seq_count // 2
    chip, core = place // 2, place % 2
    _, part_rows, width = patch_embed.shape
    local_heads, entries, _ = w_qkv.shape
    head_dim = entries // 3
    length = part_rows * seq_count
    half = length // 2
    embed, current, goal = patch_embed[0], perturbation[0], target[0]
    gain, bias = ln_gain[None], ln_bias[None]

    def swap(array, mask):
        return lax.ppermute(array, "seq", [(i, i ^ mask) for i in range(seq_count)])

    def device(chip, core, plane):
        return (chip * 2 + core) * planes + plane

    def hop(array, pairs):
        perm = [
            (device(c, *source), device(c, *dest)) for c in range(chips) for source, dest in pairs
        ]
        return lax.ppermute(array, ("seq", "head"), perm)

    def mirrored(pairs):
        flip = lambda end: (1 - end[0], planes - 1 - end[1])
        return pairs + [(flip(source), flip(dest)) for source, dest in pairs]

    first_hop = mirrored([((0, 1), (0, 0)), ((0, 0), (0, 1)), ((1, 1), (0, 2))])
    later_hops = [
        mirrored([((0, p), (0, p + 1)) for p in range(first, planes - 1)])
        for first in range(1, planes - 1)
    ]

    def chain(array):
        steps = [array, hop(array, first_hop)]
        for pairs in later_hops:
            steps.append(hop(steps[-1], pairs))
        return steps

    distance = jnp.where(core == 0, plane, planes - 1 - plane)
    depth = jnp.maximum(distance - 1, 0)

    def pick(steps, offset):
        chosen = steps[offset]
        for i in range(1, planes - 1):
            chosen = jnp.where(depth == i, steps[offset + i], chosen)
        return chosen

    qkv_steps = chain(lax.dynamic_index_in_dim(w_qkv, chip, 0, keepdims=False))
    out_steps = chain(lax.dynamic_index_in_dim(w_out, chip, 0, keepdims=False))
    w_near, w_far = pick(qkv_steps, 0), pick(qkv_steps, 1)
    out_near, out_far = pick(out_steps, 0), pick(out_steps, 1)

    (hidden,) = call(
        norm_body, [((part_rows, width), bf16)], embed, current, gain, bias, name="norm"
    )
    cut = part_rows // 2
    across = swap(hidden, 2)
    along = swap(hidden, 4)
    corner = [swap(across[:cut], 4), swap(along[cut:], 2)]
    same_core = [hidden, across, along] + corner
    other_core = [swap(part, 1) for part in same_core]

    def gather(array):
        same = [array] + [swap(array, 2 * m) for m in range(1, chips)]
        other = [swap(part, 1) for part in same]
        return [part for pair in zip(same, other) for part in pair]

    def attend(weight, name):
        square = length * length
        return call(
            functools.partial(forward_body, chips),
            [
                ((entries, length), bf16),
                ((1, length), f32),
                ((chips, head_dim, part_rows), bf16),
                ((chips, head_dim, part_rows), bf16),
            ],
            weight,
            *same_core,
            *other_core,
            flops=2 * length * entries * width + 4 * square * head_dim,
            exps=square,
            name=name,
        )

    def exchange(same, other):
        arrived = swap(other, 1)
        pairs = [jnp.stack([same[m], arrived[m]]) for m in range(chips)]
        return [pairs[0]] + [swap(pairs[m], 2 * m) for m in range(1, chips)]

    near = attend(w_near, "attend_near")
    near_slots = exchange(near[2], near[3])
    far = attend(w_far, "attend_far")
    far_slots = exchange(far[2], far[3])
    slots = [pair[j] for group in (near_slots, far_slots) for pair in group for j in range(2)]
    weights = gather(out_near) + gather(out_far)
    same_grad, other_grad, residual = call(
        functools.partial(project_body, len(slots)),
        [((chips, 2, head_dim, part_rows), bf16)] * 2 + [((part_rows, width), f32)],
        embed,
        current,
        goal,
        *slots,
        *weights,
        flops=4 * part_rows * width * width,
        name="project",
    )
    arrived = exchange(same_grad, other_grad)
    grads, swapped = [], []
    for head, (packed, total, same, other) in enumerate((near, far)):
        stay, leave = call(
            functools.partial(backward_body, head, chips),
            [((entries, half), bf16)] * 2,
            packed,
            total,
            same,
            other,
            *arrived,
            flops=10 * length * length * head_dim,
            exps=length * length,
            name="backward",
        )
        grads.append(stay)
        swapped.append(swap(leave, 1))
    both = [w_near, w_far]
    others = [swap(w, 1) for w in both]
    own, *sent = call(
        functools.partial(hidden_grad_body, 4),
        [((part_rows, width), f32)] + [((part_rows, width), bf16)] * (chips - 1),
        *grads,
        *swapped,
        *both,
        *others,
        flops=8 * half * entries * width,
        name="hidden_grad",
    )
    parts = [swap(part, 2 * (m + 1)) for m, part in enumerate(sent)]
    gradient, sums = call(
        gradient_body,
        [((part_rows, width), f32), ((8, 128), f32)],
        embed,
        current,
        residual,
        gain,
        own,
        *parts,
        name="gradient",
    )
    sums = sums + swap(sums, 1)
    sums = sums + sum(swap(sums, 2 * m) for m in range(1, chips))
    grad_square, cross, square = jnp.sum(sums, axis=1)[:3]
    rate = step_size[plane] / jnp.sqrt(grad_square + norm_epsilon)
    stepped_square = jnp.maximum(square + 2.0 * rate * cross + rate * rate * grad_square, 0.0)
    shrink = jnp.minimum(1.0, radius[plane] / jnp.sqrt(stepped_square + norm_epsilon))
    return ((current + rate * gradient) * shrink)[None]


def on_device(patch_embed, perturbation, target, ln_gain, ln_bias, w_qkv, w_out, radius, step_size):
    seq_count, planes = lax.axis_size("seq"), lax.axis_size("head")
    own_images, part_rows, _ = patch_embed.shape
    local_heads, entries, _ = w_qkv.shape
    fits = (
        own_images == 1
        and 2 * local_heads == seq_count
        and seq_count == 8
        and planes == 4
        and part_rows % 128 == 0
        and entries % 48 == 0
    )
    plan = plane_plan if fits else general_plan
    return plan(
        patch_embed, perturbation, target, ln_gain, ln_bias, w_qkv, w_out, radius, step_size
    )


def solution(mesh):
    placed = (
        P("head", "seq", None),
        P("head", "seq", None),
        P("head", "seq", None),
        P(),
        P(),
        P("head", None, None),
        P("head", None, None),
        P(),
        P(),
    )
    return jax.shard_map(
        on_device, mesh=mesh, in_specs=placed, out_specs=P("head", "seq", None), check_vma=False
    )
```

```python
import functools
import math

import jax
import jax.numpy as jnp
from jax import lax
from jax.experimental import pallas as pl
from jax.experimental.pallas import tpu as pltpu
from jax.sharding import PartitionSpec as P

norm_epsilon = 1e-06
layer_epsilon = 1e-06


def layer_statistics(gathered):
    center = gathered - jnp.mean(gathered, axis=-1, keepdims=True)
    variance = jnp.mean(center * center, axis=-1, keepdims=True)
    inverse = lax.rsqrt(variance + layer_epsilon)
    return (center * inverse, inverse)


def attend_forward(queries, key_rows, values, score_scale):
    item_count, length, head_dim = queries.shape
    block_rows = min(512, length)
    query_blocks = queries.reshape(item_count, length // block_rows, block_rows, head_dim).swapaxes(
        0, 1
    )

    def one_block(query_block):
        scores = (
            jnp.einsum("nqe,nke->nqk", query_block, key_rows, preferred_element_type=jnp.float32)
            * score_scale
        )
        row_max = jnp.max(scores, axis=-1, keepdims=True)
        log_total = row_max + jnp.log(jnp.sum(jnp.exp(scores - row_max), axis=-1, keepdims=True))
        weights = jnp.exp(scores - log_total).astype(jnp.bfloat16)
        output = jnp.einsum(
            "nqk,nke->nqe", weights, values, preferred_element_type=jnp.float32
        ).astype(jnp.bfloat16)
        return (output, log_total[..., 0])

    output, log_total = lax.map(one_block, query_blocks)
    output = output.swapaxes(0, 1).reshape(item_count, length, head_dim)
    log_total = log_total.swapaxes(0, 1).reshape(item_count, length)
    return (output, log_total)


def attend_backward(queries, key_rows, values, output, log_total, grad_output, score_scale):
    item_count, length, head_dim = queries.shape
    block_rows = min(512, length)
    block_count = length // block_rows

    def cut_rows(array):
        return array.reshape((item_count, block_count, block_rows) + array.shape[2:]).swapaxes(0, 1)

    row_dot = jnp.sum(grad_output.astype(jnp.float32) * output.astype(jnp.float32), axis=-1)

    def one_block(carry, inputs):
        grad_keys, grad_values = carry
        query_block, grad_block, total_block, dot_block = inputs
        scores = (
            jnp.einsum("nqe,nke->nqk", query_block, key_rows, preferred_element_type=jnp.float32)
            * score_scale
        )
        weights = jnp.exp(scores - total_block[..., None])
        grad_values = grad_values + jnp.einsum(
            "nqk,nqe->nke",
            weights.astype(jnp.bfloat16),
            grad_block,
            preferred_element_type=jnp.float32,
        )
        grad_weights = jnp.einsum(
            "nqe,nke->nqk", grad_block, values, preferred_element_type=jnp.float32
        )
        grad_scores = (weights * (grad_weights - dot_block[..., None]) * score_scale).astype(
            jnp.bfloat16
        )
        grad_query = jnp.einsum(
            "nqk,nke->nqe", grad_scores, key_rows, preferred_element_type=jnp.float32
        ).astype(jnp.bfloat16)
        grad_keys = grad_keys + jnp.einsum(
            "nqk,nqe->nke", grad_scores, query_block, preferred_element_type=jnp.float32
        )
        return ((grad_keys, grad_values), grad_query)

    zero_rows = jnp.zeros((item_count, length, head_dim), jnp.float32)
    (grad_keys, grad_values), grad_query = lax.scan(
        one_block,
        (zero_rows, zero_rows),
        (cut_rows(queries), cut_rows(grad_output), cut_rows(log_total), cut_rows(row_dot)),
    )
    grad_query = grad_query.swapaxes(0, 1).reshape(item_count, length, head_dim)
    return jnp.concatenate(
        [grad_query, grad_keys.astype(jnp.bfloat16), grad_values.astype(jnp.bfloat16)], axis=-1
    )


def general_plan(patch_embed, perturbation, target, ln_gain, ln_bias, w_qkv, w_out, radius, step_size):
    seq_count = lax.axis_size("seq")
    own_images, part_rows, _ = patch_embed.shape
    local_heads = w_qkv.shape[0]
    head_dim = w_qkv.shape[1] // 3
    examples = own_images * lax.axis_size("head")
    pair_count = examples * local_heads // seq_count
    first_image = lax.axis_index("head") * own_images
    own_step = lax.dynamic_slice_in_dim(step_size, first_image, own_images, 0)
    own_radius = lax.dynamic_slice_in_dim(radius, first_image, own_images, 0)
    score_scale = 1.0 / math.sqrt(head_dim)
    current = perturbation
    mixed = patch_embed.astype(jnp.float32) + current
    rounded = mixed.astype(jnp.bfloat16)
    normed, inverse = layer_statistics(rounded.astype(jnp.float32))
    hidden = (normed * ln_gain + ln_bias).astype(jnp.bfloat16)
    hidden_all = lax.all_gather(hidden, "head", axis=0, tiled=True)
    packed = jnp.einsum(
        "epd,hcd->ehpc", hidden_all, w_qkv, preferred_element_type=jnp.float32
    ).astype(jnp.bfloat16)
    packed = packed.reshape(seq_count, pair_count, part_rows, 3 * head_dim)
    pair_rows = lax.all_to_all(packed, "seq", split_axis=0, concat_axis=2, tiled=True)[0]
    queries = pair_rows[..., :head_dim]
    key_rows = pair_rows[..., head_dim : 2 * head_dim]
    values = pair_rows[..., 2 * head_dim :]
    output, log_total = attend_forward(queries, key_rows, values, score_scale)
    returned = lax.all_to_all(output[None], "seq", split_axis=2, concat_axis=0, tiled=True)
    returned = returned.reshape(examples, local_heads, part_rows, head_dim)
    partial_value = jnp.einsum("ehpc,hcd->epd", returned, w_out, preferred_element_type=jnp.float32)
    branch = lax.psum_scatter(partial_value, "head", scatter_dimension=0, tiled=True)
    result = mixed + branch
    residual = result - target.astype(jnp.float32)
    residual_all = lax.all_gather(residual.astype(jnp.bfloat16), "head", axis=0, tiled=True)
    grad_output = jnp.einsum(
        "epd,hcd->ehpc", residual_all, w_out, preferred_element_type=jnp.float32
    ).astype(jnp.bfloat16)
    grad_output = grad_output.reshape(seq_count, pair_count, part_rows, head_dim)
    grad_pairs = lax.all_to_all(grad_output, "seq", split_axis=0, concat_axis=2, tiled=True)[0]
    grad_packed = attend_backward(
        queries, key_rows, values, output, log_total, grad_pairs, score_scale
    )
    grad_tokens = lax.all_to_all(grad_packed[None], "seq", split_axis=2, concat_axis=0, tiled=True)
    grad_tokens = grad_tokens.reshape(examples, local_heads, part_rows, 3 * head_dim)
    grad_partial = jnp.einsum(
        "ehpc,hcd->epd", grad_tokens, w_qkv, preferred_element_type=jnp.float32
    )
    grad_hidden = lax.psum_scatter(grad_partial, "head", scatter_dimension=0, tiled=True)
    scaled = grad_hidden * ln_gain
    first_mean = jnp.mean(scaled, axis=-1, keepdims=True)
    second_mean = jnp.mean(scaled * normed, axis=-1, keepdims=True)
    grad_input = (scaled - first_mean - normed * second_mean) * inverse
    gradient = residual + grad_input
    grad_square = lax.psum(jnp.sum(gradient * gradient, axis=(1, 2)), "seq")
    stepped = current + (own_step / jnp.sqrt(grad_square + norm_epsilon))[:, None, None] * gradient
    stepped_square = lax.psum(jnp.sum(stepped * stepped, axis=(1, 2)), "seq")
    current = (
        stepped
        * jnp.minimum(1.0, own_radius / jnp.sqrt(stepped_square + norm_epsilon))[:, None, None]
    )
    return current


LOG2E = math.log2(math.e)
bf16 = jnp.bfloat16
f32 = jnp.float32
VMEM = pl.BlockSpec(memory_space=pltpu.VMEM)
SMEM = pl.BlockSpec(memory_space=pltpu.SMEM)


def dot(a, b, a_dim, b_dim):
    return lax.dot_general(a, b, (((a_dim,), (b_dim,)), ((), ())), preferred_element_type=f32)


def call(body, outs, *args, scalars=0, flops=0, exps=0):
    shapes = [jax.ShapeDtypeStruct(shape, dtype) for shape, dtype in outs]
    moved = sum(a.size * a.dtype.itemsize for a in list(args) + shapes)
    return pl.pallas_call(
        body,
        out_shape=shapes,
        in_specs=[SMEM] * scalars + [VMEM] * (len(args) - scalars),
        out_specs=[VMEM] * len(shapes),
        cost_estimate=pl.CostEstimate(flops=flops, transcendentals=exps, bytes_accessed=moved),
        compiler_params=pltpu.CompilerParams(vmem_limit_bytes=24 << 20),
    )(*args)


def norm_parts(embed, current):
    rounded = (embed.astype(f32) + current).astype(bf16).astype(f32)
    center = rounded - jnp.mean(rounded, axis=-1, keepdims=True)
    inverse = lax.rsqrt(jnp.mean(center * center, axis=-1, keepdims=True) + layer_epsilon)
    return center * inverse, inverse


def norm_body(embed, current, gain, bias, hidden):
    normed, _ = norm_parts(embed[...], current[...])
    hidden[...] = (normed * gain[...][None] + bias[...][None]).astype(bf16)


def forward_body(places, choices, merge, depth_ref, *refs):
    candidates, refs = refs[:choices], refs[choices:]
    hidden, refs = refs[:places], refs[places:]
    if merge:
        earlier, refs = refs[0], refs[1:]
    packed_ref, total_ref, weight_ref, out_ref, *joined = refs
    depth = depth_ref[0]
    weight = candidates[0][...]
    for i in range(1, choices):
        weight = jnp.where(depth == i, candidates[i][...], weight)
    weight_ref[...] = weight
    entries, _ = weight.shape
    head_dim = entries // 3
    rows = hidden[0].shape[0]
    length = packed_ref.shape[1]
    scale = LOG2E / math.sqrt(head_dim)
    for i in range(0, places, 2):
        rhs = jnp.concatenate([hidden[i][...], hidden[i + 1][...]], axis=0)
        packed_ref[:, i * rows : (i + 2) * rows] = dot(weight_ref[...], rhs, 1, 1).astype(bf16)
    keys = packed_ref[head_dim : 2 * head_dim, :].T
    values_t = packed_ref[2 * head_dim :, :]
    step = min(256, length)
    for q in range(0, length, step):
        queries_t = packed_ref[:head_dim, q : q + step]
        scores = dot(keys, queries_t, 1, 0) * scale
        top = jnp.max(scores, axis=0, keepdims=True)
        raised = jnp.exp2(scores - top)
        total = jnp.sum(raised, axis=0, keepdims=True)
        total_ref[:, q : q + step] = top + jnp.log2(total)
        out = (dot(values_t, raised.astype(bf16), 1, 0) * (1.0 / total)).astype(bf16)
        out_ref[:, q : q + step] = out
    for i, dest in enumerate(joined):
        cut = slice(i * rows, (i + 1) * rows)
        dest[:head_dim, :] = earlier[:, cut]
        dest[head_dim:, :] = out_ref[:, cut]


def project_body(slots, embed, current, target, *refs):
    outs, weights = refs[:slots], refs[slots : 2 * slots]
    *grad_refs, residual_ref = refs[2 * slots :]
    outs_t = jnp.concatenate([o[...] for o in outs], axis=0)
    full = jnp.concatenate([w[...] for w in weights], axis=0)
    branch = dot(outs_t, full, 0, 0)
    residual = embed[...].astype(f32) + current[...] + branch - target[...].astype(f32)
    residual_ref[...] = residual
    grads = dot(full, residual.astype(bf16), 1, 1).astype(bf16)
    size = grad_refs[0].shape[0]
    for i, dest in enumerate(grad_refs):
        dest[...] = grads[i * size : (i + 1) * size, :]


def backward_body(head, packed_ref, total_ref, out_ref, *refs):
    arrived, (same_grad, other_grad) = refs[:-2], refs[-2:]
    entries, length = packed_ref.shape
    head_dim = entries // 3
    scale = 1.0 / math.sqrt(head_dim)
    cut = slice(head * head_dim, (head + 1) * head_dim)
    grads_t = jnp.concatenate([part[cut, :] for part in arrived], axis=1)
    out_t = out_ref[...]
    queries_t = packed_ref[:head_dim, :]
    keys_t = packed_ref[head_dim : 2 * head_dim, :]
    keys = keys_t.T
    values = packed_ref[2 * head_dim :, :].T
    row_dot = jnp.sum(grads_t.astype(f32) * out_t.astype(f32), axis=0, keepdims=True)
    step = min(256, length)
    grad_keys = jnp.zeros((head_dim, length), f32)
    grad_values = jnp.zeros((head_dim, length), f32)
    half = length // 2
    for q in range(0, length, step):
        cut = slice(q, q + step)
        scores = dot(keys, queries_t[:, cut], 1, 0) * (scale * LOG2E)
        weights = jnp.exp2(scores - total_ref[:, cut])
        grad_weights = dot(values, grads_t[:, cut], 1, 0)
        grad_scores = (weights * (grad_weights - row_dot[:, cut]) * scale).astype(bf16)
        grad_values = grad_values + dot(grads_t[:, cut], weights.astype(bf16), 1, 1)
        grad_keys = grad_keys + dot(queries_t[:, cut], grad_scores, 1, 1)
        grad_query = dot(keys_t, grad_scores, 1, 0).astype(bf16)
        dest = same_grad if q < half else other_grad
        dest[:head_dim, q % half : q % half + step] = grad_query
    for i, dest in enumerate((same_grad, other_grad)):
        dest[head_dim : 2 * head_dim, :] = grad_keys[:, i * half : (i + 1) * half].astype(bf16)
        dest[2 * head_dim :, :] = grad_values[:, i * half : (i + 1) * half].astype(bf16)


def hidden_grad_body(count, *refs):
    grads, weights = refs[:count], refs[count : 2 * count]
    own, sent = refs[2 * count], refs[2 * count + 1 :]
    rows = own.shape[0]
    total = sum(dot(g[...], w[...], 0, 0) for g, w in zip(grads, weights))
    own[...] = total[:rows]
    for i, dest in enumerate(sent):
        dest[...] = total[(i + 1) * rows : (i + 2) * rows].astype(bf16)


def gradient_body(embed, current, residual, gain, own, *refs):
    arrived, (gradient_ref, sums_ref) = refs[:-2], refs[-2:]
    grad_hidden = own[...]
    for part in arrived:
        grad_hidden = grad_hidden + part[...].astype(f32)
    normed, inverse = norm_parts(embed[...], current[...])
    scaled = grad_hidden * gain[...][None]
    first_mean = jnp.mean(scaled, axis=-1, keepdims=True)
    second_mean = jnp.mean(scaled * normed, axis=-1, keepdims=True)
    gradient = residual[...] + (scaled - first_mean - normed * second_mean) * inverse
    gradient_ref[...] = gradient
    before = current[...]
    lanes = sums_ref.shape[1]
    sums_ref[...] = jnp.zeros_like(sums_ref)
    for i, terms in enumerate((gradient * gradient, before * gradient, before * before)):
        columns = jnp.sum(terms, axis=0, keepdims=True)
        sums_ref[i : i + 1, :] = sum(
            columns[:, j : j + lanes] for j in range(0, columns.shape[1], lanes)
        )


def finish_body(plane_ref, step_ref, radius_ref, *refs):
    *sum_refs, current, gradient, moved = refs
    sums = jnp.sum(sum(ref[...] for ref in sum_refs), axis=1, keepdims=True)
    grad_square, cross, square = sums[0:1], sums[1:2], sums[2:3]
    plane = plane_ref[0]
    rate = step_ref[plane] / jnp.sqrt(grad_square + norm_epsilon)
    stepped_square = jnp.maximum(square + 2.0 * rate * cross + rate * rate * grad_square, 0.0)
    shrink = jnp.minimum(1.0, radius_ref[plane] / jnp.sqrt(stepped_square + norm_epsilon))
    moved[...] = (current[...] + rate * gradient[...]) * shrink


def plane_plan(patch_embed, perturbation, target, ln_gain, ln_bias, w_qkv, w_out, radius, step_size):
    seq_count, planes = lax.axis_size("seq"), lax.axis_size("head")
    place, plane = lax.axis_index("seq"), lax.axis_index("head")
    chips = seq_count // 2
    chip, core = place // 2, place % 2
    _, part_rows, width = patch_embed.shape
    _, entries, _ = w_qkv.shape
    head_dim = entries // 3
    length = part_rows * seq_count
    half = length // 2
    embed, current, goal = patch_embed[0], perturbation[0], target[0]

    def swap(array, mask):
        return lax.ppermute(array, "seq", [(i, i ^ mask) for i in range(seq_count)])

    def device(chip, core, plane):
        return (chip * 2 + core) * planes + plane

    def hop(array, pairs):
        perm = [
            (device(c, *source), device(c, *dest)) for c in range(chips) for source, dest in pairs
        ]
        return lax.ppermute(array, ("seq", "head"), perm)

    def mirrored(pairs):
        flip = lambda end: (1 - end[0], planes - 1 - end[1])
        return pairs + [(flip(source), flip(dest)) for source, dest in pairs]

    first_hop = mirrored([((0, 1), (0, 0)), ((0, 0), (0, 1)), ((1, 1), (0, 2))])
    later_hops = [
        mirrored([((0, p), (0, p + 1)) for p in range(first, planes - 1)])
        for first in range(1, planes - 1)
    ]

    def chain(array):
        steps = [array, hop(array, first_hop)]
        for pairs in later_hops:
            steps.append(hop(steps[-1], pairs))
        return steps

    distance = jnp.where(core == 0, plane, planes - 1 - plane)
    depth = jnp.maximum(distance - 1, 0)

    def pick(steps):
        chosen = steps[0]
        for i in range(1, len(steps)):
            chosen = jnp.where(depth == i, steps[i], chosen)
        return chosen

    qkv_steps = chain(lax.dynamic_index_in_dim(w_qkv, chip, 0, keepdims=False))
    out_steps = chain(lax.dynamic_index_in_dim(w_out, chip, 0, keepdims=False))
    (hidden,) = call(norm_body, [((part_rows, width), bf16)], embed, current, ln_gain, ln_bias)

    masks = [2 * m + j for j in range(2) for m in range(chips)]

    def gather(array):
        same = [array] + [swap(array, 2 * m) for m in range(1, chips)]
        return same + [swap(part, 1) for part in same]

    def exchange(parts):
        return [parts[0]] + [swap(part, mask) for part, mask in zip(parts[1:], masks[1:])]

    hidden_rows = gather(hidden)

    def attend(steps, earlier=()):
        square = length * length
        joined = [((2 * head_dim, part_rows), bf16)] * (seq_count if earlier else 0)
        return call(
            functools.partial(forward_body, seq_count, len(steps), bool(earlier)),
            [
                ((entries, length), bf16),
                ((1, length), f32),
                ((entries, width), bf16),
                ((head_dim, length), bf16),
            ]
            + joined,
            depth.reshape(1),
            *steps,
            *hidden_rows,
            *earlier,
            scalars=1,
            flops=2 * length * entries * width + 4 * square * head_dim,
            exps=square,
        )

    near = attend(qkv_steps[:-1])
    far = attend(qkv_steps[1:], near[3:4])
    slots = exchange(far[4:])
    out_own = jnp.concatenate([pick(out_steps[:-1]), pick(out_steps[1:])], axis=0)
    weights = gather(out_own)
    *grad_parts, residual = call(
        functools.partial(project_body, len(slots)),
        [((2 * head_dim, part_rows), bf16)] * seq_count + [((part_rows, width), f32)],
        embed,
        current,
        goal,
        *slots,
        *weights,
        flops=4 * part_rows * width * width,
    )
    arrived = exchange(grad_parts)
    grads, swapped = [], []
    for head, (packed, total, _, out, *_) in enumerate((near, far)):
        stay, leave = call(
            functools.partial(backward_body, head),
            [((entries, half), bf16)] * 2,
            packed,
            total,
            out,
            *arrived,
            flops=10 * length * length * head_dim,
            exps=length * length,
        )
        grads.append(stay)
        swapped.append(swap(leave, 1))
    both = [near[2], far[2]]
    others = [swap(w, 1) for w in both]
    own, *sent = call(
        functools.partial(hidden_grad_body, 4),
        [((part_rows, width), f32)] + [((part_rows, width), bf16)] * (chips - 1),
        *grads,
        *swapped,
        *both,
        *others,
        flops=8 * half * entries * width,
    )
    parts = [swap(part, 2 * (m + 1)) for m, part in enumerate(sent)]
    gradient, sums = call(
        gradient_body,
        [((part_rows, width), f32), ((8, 128), f32)],
        embed,
        current,
        residual,
        ln_gain,
        own,
        *parts,
    )
    sums = sums + swap(sums, 1)
    (moved,) = call(
        finish_body,
        [((part_rows, width), f32)],
        plane.reshape(1),
        step_size,
        radius,
        sums,
        *[swap(sums, 2 * m) for m in range(1, chips)],
        current,
        gradient,
        scalars=3,
    )
    return moved[None]


def on_device(patch_embed, perturbation, target, ln_gain, ln_bias, w_qkv, w_out, radius, step_size):
    seq_count, planes = lax.axis_size("seq"), lax.axis_size("head")
    own_images, part_rows, _ = patch_embed.shape
    local_heads, entries, _ = w_qkv.shape
    fits = (
        own_images == 1
        and 2 * local_heads == seq_count
        and seq_count == 8
        and planes == 4
        and part_rows % 128 == 0
        and entries % 48 == 0
    )
    plan = plane_plan if fits else general_plan
    return plan(
        patch_embed, perturbation, target, ln_gain, ln_bias, w_qkv, w_out, radius, step_size
    )


def solution(mesh):
    placed = (
        P("head", "seq", None),
        P("head", "seq", None),
        P("head", "seq", None),
        P(),
        P(),
        P("head", None, None),
        P("head", None, None),
        P(),
        P(),
    )
    return jax.shard_map(
        on_device, mesh=mesh, in_specs=placed, out_specs=P("head", "seq", None), check_vma=False
    )
```

```python
import functools
import math

import jax
import jax.numpy as jnp
from jax import lax
from jax.experimental import pallas as pl
from jax.experimental.pallas import tpu as pltpu
from jax.sharding import PartitionSpec as P

norm_epsilon = 1e-06
layer_epsilon = 1e-06


def layer_statistics(gathered):
    center = gathered - jnp.mean(gathered, axis=-1, keepdims=True)
    variance = jnp.mean(center * center, axis=-1, keepdims=True)
    inverse = lax.rsqrt(variance + layer_epsilon)
    return (center * inverse, inverse)


def attend_forward(queries, key_rows, values, score_scale):
    item_count, length, head_dim = queries.shape
    block_rows = min(512, length)
    query_blocks = queries.reshape(item_count, length // block_rows, block_rows, head_dim).swapaxes(
        0, 1
    )

    def one_block(query_block):
        scores = (
            jnp.einsum("nqe,nke->nqk", query_block, key_rows, preferred_element_type=jnp.float32)
            * score_scale
        )
        row_max = jnp.max(scores, axis=-1, keepdims=True)
        log_total = row_max + jnp.log(jnp.sum(jnp.exp(scores - row_max), axis=-1, keepdims=True))
        weights = jnp.exp(scores - log_total).astype(jnp.bfloat16)
        output = jnp.einsum(
            "nqk,nke->nqe", weights, values, preferred_element_type=jnp.float32
        ).astype(jnp.bfloat16)
        return (output, log_total[..., 0])

    output, log_total = lax.map(one_block, query_blocks)
    output = output.swapaxes(0, 1).reshape(item_count, length, head_dim)
    log_total = log_total.swapaxes(0, 1).reshape(item_count, length)
    return (output, log_total)


def attend_backward(queries, key_rows, values, output, log_total, grad_output, score_scale):
    item_count, length, head_dim = queries.shape
    block_rows = min(512, length)
    block_count = length // block_rows

    def cut_rows(array):
        return array.reshape((item_count, block_count, block_rows) + array.shape[2:]).swapaxes(0, 1)

    row_dot = jnp.sum(grad_output.astype(jnp.float32) * output.astype(jnp.float32), axis=-1)

    def one_block(carry, inputs):
        grad_keys, grad_values = carry
        query_block, grad_block, total_block, dot_block = inputs
        scores = (
            jnp.einsum("nqe,nke->nqk", query_block, key_rows, preferred_element_type=jnp.float32)
            * score_scale
        )
        weights = jnp.exp(scores - total_block[..., None])
        grad_values = grad_values + jnp.einsum(
            "nqk,nqe->nke",
            weights.astype(jnp.bfloat16),
            grad_block,
            preferred_element_type=jnp.float32,
        )
        grad_weights = jnp.einsum(
            "nqe,nke->nqk", grad_block, values, preferred_element_type=jnp.float32
        )
        grad_scores = (weights * (grad_weights - dot_block[..., None]) * score_scale).astype(
            jnp.bfloat16
        )
        grad_query = jnp.einsum(
            "nqk,nke->nqe", grad_scores, key_rows, preferred_element_type=jnp.float32
        ).astype(jnp.bfloat16)
        grad_keys = grad_keys + jnp.einsum(
            "nqk,nqe->nke", grad_scores, query_block, preferred_element_type=jnp.float32
        )
        return ((grad_keys, grad_values), grad_query)

    zero_rows = jnp.zeros((item_count, length, head_dim), jnp.float32)
    (grad_keys, grad_values), grad_query = lax.scan(
        one_block,
        (zero_rows, zero_rows),
        (cut_rows(queries), cut_rows(grad_output), cut_rows(log_total), cut_rows(row_dot)),
    )
    grad_query = grad_query.swapaxes(0, 1).reshape(item_count, length, head_dim)
    return jnp.concatenate(
        [grad_query, grad_keys.astype(jnp.bfloat16), grad_values.astype(jnp.bfloat16)], axis=-1
    )


def general_plan(patch_embed, perturbation, target, ln_gain, ln_bias, w_qkv, w_out, radius, step_size):
    seq_count = lax.axis_size("seq")
    own_images, part_rows, _ = patch_embed.shape
    local_heads = w_qkv.shape[0]
    head_dim = w_qkv.shape[1] // 3
    examples = own_images * lax.axis_size("head")
    pair_count = examples * local_heads // seq_count
    first_image = lax.axis_index("head") * own_images
    own_step = lax.dynamic_slice_in_dim(step_size, first_image, own_images, 0)
    own_radius = lax.dynamic_slice_in_dim(radius, first_image, own_images, 0)
    score_scale = 1.0 / math.sqrt(head_dim)
    current = perturbation
    mixed = patch_embed.astype(jnp.float32) + current
    rounded = mixed.astype(jnp.bfloat16)
    normed, inverse = layer_statistics(rounded.astype(jnp.float32))
    hidden = (normed * ln_gain + ln_bias).astype(jnp.bfloat16)
    hidden_all = lax.all_gather(hidden, "head", axis=0, tiled=True)
    packed = jnp.einsum(
        "epd,hcd->ehpc", hidden_all, w_qkv, preferred_element_type=jnp.float32
    ).astype(jnp.bfloat16)
    packed = packed.reshape(seq_count, pair_count, part_rows, 3 * head_dim)
    pair_rows = lax.all_to_all(packed, "seq", split_axis=0, concat_axis=2, tiled=True)[0]
    queries = pair_rows[..., :head_dim]
    key_rows = pair_rows[..., head_dim : 2 * head_dim]
    values = pair_rows[..., 2 * head_dim :]
    output, log_total = attend_forward(queries, key_rows, values, score_scale)
    returned = lax.all_to_all(output[None], "seq", split_axis=2, concat_axis=0, tiled=True)
    returned = returned.reshape(examples, local_heads, part_rows, head_dim)
    partial_value = jnp.einsum("ehpc,hcd->epd", returned, w_out, preferred_element_type=jnp.float32)
    branch = lax.psum_scatter(partial_value, "head", scatter_dimension=0, tiled=True)
    result = mixed + branch
    residual = result - target.astype(jnp.float32)
    residual_all = lax.all_gather(residual.astype(jnp.bfloat16), "head", axis=0, tiled=True)
    grad_output = jnp.einsum(
        "epd,hcd->ehpc", residual_all, w_out, preferred_element_type=jnp.float32
    ).astype(jnp.bfloat16)
    grad_output = grad_output.reshape(seq_count, pair_count, part_rows, head_dim)
    grad_pairs = lax.all_to_all(grad_output, "seq", split_axis=0, concat_axis=2, tiled=True)[0]
    grad_packed = attend_backward(
        queries, key_rows, values, output, log_total, grad_pairs, score_scale
    )
    grad_tokens = lax.all_to_all(grad_packed[None], "seq", split_axis=2, concat_axis=0, tiled=True)
    grad_tokens = grad_tokens.reshape(examples, local_heads, part_rows, 3 * head_dim)
    grad_partial = jnp.einsum(
        "ehpc,hcd->epd", grad_tokens, w_qkv, preferred_element_type=jnp.float32
    )
    grad_hidden = lax.psum_scatter(grad_partial, "head", scatter_dimension=0, tiled=True)
    scaled = grad_hidden * ln_gain
    first_mean = jnp.mean(scaled, axis=-1, keepdims=True)
    second_mean = jnp.mean(scaled * normed, axis=-1, keepdims=True)
    grad_input = (scaled - first_mean - normed * second_mean) * inverse
    gradient = residual + grad_input
    grad_square = lax.psum(jnp.sum(gradient * gradient, axis=(1, 2)), "seq")
    stepped = current + (own_step / jnp.sqrt(grad_square + norm_epsilon))[:, None, None] * gradient
    stepped_square = lax.psum(jnp.sum(stepped * stepped, axis=(1, 2)), "seq")
    current = (
        stepped
        * jnp.minimum(1.0, own_radius / jnp.sqrt(stepped_square + norm_epsilon))[:, None, None]
    )
    return current


LOG2E = math.log2(math.e)
bf16 = jnp.bfloat16
f32 = jnp.float32
VMEM = pl.BlockSpec(memory_space=pltpu.VMEM)
SMEM = pl.BlockSpec(memory_space=pltpu.SMEM)
HBM = pl.BlockSpec(memory_space=pltpu.HBM)
VMEM_LIMIT = 24 << 20


def dot(a, b, a_dim, b_dim):
    return lax.dot_general(a, b, (((a_dim,), (b_dim,)), ((), ())), preferred_element_type=f32)


def call(body, outs, *args, scalars=0, flops=0, exps=0):
    shapes = [jax.ShapeDtypeStruct(shape, dtype) for shape, dtype in outs]
    moved = sum(a.size * a.dtype.itemsize for a in list(args) + shapes)
    return pl.pallas_call(
        body,
        out_shape=shapes,
        in_specs=[SMEM] * scalars + [VMEM] * (len(args) - scalars),
        out_specs=[VMEM] * len(shapes),
        cost_estimate=pl.CostEstimate(flops=flops, transcendentals=exps, bytes_accessed=moved),
        compiler_params=pltpu.CompilerParams(vmem_limit_bytes=VMEM_LIMIT),
    )(*args)


def norm_parts(embed, current):
    rounded = (embed.astype(f32) + current).astype(bf16).astype(f32)
    center = rounded - jnp.mean(rounded, axis=-1, keepdims=True)
    inverse = lax.rsqrt(jnp.mean(center * center, axis=-1, keepdims=True) + layer_epsilon)
    return center * inverse, inverse


def begin_body(chip_ref, embed, current, gain, bias, qkv, out, hidden, upper, lower, *scratch):
    *held, sems = scratch
    chip = chip_ref[0]
    head_dim = out.shape[1]
    pairs = list(zip((embed, current, gain, bias), held))
    pairs += [
        (qkv.at[chip, pl.ds(0, 2 * head_dim)], upper),
        (qkv.at[chip, pl.ds(2 * head_dim, head_dim)], lower.at[pl.ds(0, head_dim)]),
        (out.at[chip], lower.at[pl.ds(head_dim, head_dim)]),
    ]
    copies = [
        pltpu.make_async_copy(source, dest, sems.at[i]) for i, (source, dest) in enumerate(pairs)
    ]
    for copy in copies:
        copy.start()
    for copy in copies[:4]:
        copy.wait()
    embed, current, gain, bias = held
    normed, _ = norm_parts(embed[...], current[...])
    hidden[...] = (normed * gain[...][None] + bias[...][None]).astype(bf16)
    for copy in copies[4:]:
        copy.wait()


def pick(depth, steps, cut):
    value = steps[0][cut, :]
    for i in range(1, len(steps)):
        value = jnp.where(depth == i, steps[i][cut, :], value)
    return value


def pick_body(depth_ref, *refs):
    steps, chosen = refs[:-1], refs[-1]
    size = chosen.shape[0] // 2
    cut = slice(size, 2 * size)
    chosen[:size, :] = pick(depth_ref[0], steps[:-1], cut)
    chosen[size:, :] = pick(depth_ref[0], steps[1:], cut)


def forward_body(places, choices, merge, depth_ref, *refs):
    uppers, lowers, refs = refs[:choices], refs[choices : 2 * choices], refs[2 * choices :]
    hidden, refs = refs[:places], refs[places:]
    if merge:
        earlier, refs = refs[0], refs[1:]
    packed_ref, total_ref, weight_ref, out_ref, *joined = refs
    depth = depth_ref[0]
    entries, _ = weight_ref.shape
    head_dim = entries // 3
    weight_ref[: 2 * head_dim, :] = pick(depth, uppers, slice(0, 2 * head_dim))
    weight_ref[2 * head_dim :, :] = pick(depth, lowers, slice(0, head_dim))
    rows = hidden[0].shape[0]
    length = packed_ref.shape[1]
    scale = LOG2E / math.sqrt(head_dim)
    for i in range(0, places, 2):
        rhs = jnp.concatenate([hidden[i][...], hidden[i + 1][...]], axis=0)
        packed_ref[:, i * rows : (i + 2) * rows] = dot(weight_ref[...], rhs, 1, 1).astype(bf16)
    keys = packed_ref[head_dim : 2 * head_dim, :].T
    values_t = packed_ref[2 * head_dim :, :]
    step = min(256, length)
    for q in range(0, length, step):
        queries_t = packed_ref[:head_dim, q : q + step]
        scores = dot(keys, queries_t, 1, 0) * scale
        top = jnp.max(scores, axis=0, keepdims=True)
        raised = jnp.exp2(scores - top)
        total = jnp.sum(raised, axis=0, keepdims=True)
        total_ref[:, q : q + step] = top + jnp.log2(total)
        out = (dot(values_t, raised.astype(bf16), 1, 0) * (1.0 / total)).astype(bf16)
        out_ref[:, q : q + step] = out
    for i, dest in enumerate(joined):
        cut = slice(i * rows, (i + 1) * rows)
        dest[:head_dim, :] = earlier[:, cut]
        dest[head_dim:, :] = out_ref[:, cut]


def project_body(slots, embed, current, target, *refs):
    outs, weights = refs[:slots], refs[slots : 2 * slots]
    *grad_refs, residual_ref = refs[2 * slots :]
    outs_t = jnp.concatenate([o[...] for o in outs], axis=0)
    full = jnp.concatenate([w[...] for w in weights], axis=0)
    branch = dot(outs_t, full, 0, 0)
    residual = embed[...].astype(f32) + current[...] + branch - target[...].astype(f32)
    residual_ref[...] = residual
    grads = dot(full, residual.astype(bf16), 1, 1).astype(bf16)
    size = grad_refs[0].shape[0]
    for i, dest in enumerate(grad_refs):
        dest[...] = grads[i * size : (i + 1) * size, :]


def backward_body(head, packed_ref, total_ref, out_ref, *refs):
    arrived, (same_grad, other_grad) = refs[:-2], refs[-2:]
    entries, length = packed_ref.shape
    head_dim = entries // 3
    scale = 1.0 / math.sqrt(head_dim)
    cut = slice(head * head_dim, (head + 1) * head_dim)
    grads_t = jnp.concatenate([part[cut, :] for part in arrived], axis=1)
    out_t = out_ref[...]
    queries_t = packed_ref[:head_dim, :]
    keys_t = packed_ref[head_dim : 2 * head_dim, :]
    keys = keys_t.T
    values = packed_ref[2 * head_dim :, :].T
    row_dot = jnp.sum(grads_t.astype(f32) * out_t.astype(f32), axis=0, keepdims=True)
    step = min(256, length)
    grad_keys = jnp.zeros((head_dim, length), f32)
    grad_values = jnp.zeros((head_dim, length), f32)
    half = length // 2
    for q in range(0, length, step):
        cut = slice(q, q + step)
        scores = dot(keys, queries_t[:, cut], 1, 0) * (scale * LOG2E)
        weights = jnp.exp2(scores - total_ref[:, cut])
        grad_weights = dot(values, grads_t[:, cut], 1, 0)
        grad_scores = (weights * (grad_weights - row_dot[:, cut]) * scale).astype(bf16)
        grad_values = grad_values + dot(grads_t[:, cut], weights.astype(bf16), 1, 1)
        grad_keys = grad_keys + dot(queries_t[:, cut], grad_scores, 1, 1)
        grad_query = dot(keys_t, grad_scores, 1, 0).astype(bf16)
        dest = same_grad if q < half else other_grad
        dest[:head_dim, q % half : q % half + step] = grad_query
    for i, dest in enumerate((same_grad, other_grad)):
        dest[head_dim : 2 * head_dim, :] = grad_keys[:, i * half : (i + 1) * half].astype(bf16)
        dest[2 * head_dim :, :] = grad_values[:, i * half : (i + 1) * half].astype(bf16)


def hidden_grad_body(count, *refs):
    grads, weights = refs[:count], refs[count : 2 * count]
    own, sent = refs[2 * count], refs[2 * count + 1 :]
    rows = own.shape[0]
    total = sum(dot(g[...], w[...], 0, 0) for g, w in zip(grads, weights))
    own[...] = total[:rows]
    for i, dest in enumerate(sent):
        dest[...] = total[(i + 1) * rows : (i + 2) * rows].astype(bf16)


def gradient_body(embed, current, residual, gain, own, *refs):
    arrived, (gradient_ref, sums_ref) = refs[:-2], refs[-2:]
    grad_hidden = own[...]
    for part in arrived:
        grad_hidden = grad_hidden + part[...].astype(f32)
    normed, inverse = norm_parts(embed[...], current[...])
    scaled = grad_hidden * gain[...][None]
    first_mean = jnp.mean(scaled, axis=-1, keepdims=True)
    second_mean = jnp.mean(scaled * normed, axis=-1, keepdims=True)
    gradient = residual[...] + (scaled - first_mean - normed * second_mean) * inverse
    gradient_ref[...] = gradient
    before = current[...]
    lanes = sums_ref.shape[1]
    sums_ref[...] = jnp.zeros_like(sums_ref)
    for i, terms in enumerate((gradient * gradient, before * gradient, before * before)):
        columns = jnp.sum(terms, axis=0, keepdims=True)
        sums_ref[i : i + 1, :] = sum(
            columns[:, j : j + lanes] for j in range(0, columns.shape[1], lanes)
        )


def finish_body(plane_ref, step_ref, radius_ref, *refs):
    *sum_refs, current, gradient, moved = refs
    sums = jnp.sum(sum(ref[...] for ref in sum_refs), axis=1, keepdims=True)
    grad_square, cross, square = sums[0:1], sums[1:2], sums[2:3]
    plane = plane_ref[0]
    rate = step_ref[plane] / jnp.sqrt(grad_square + norm_epsilon)
    stepped_square = jnp.maximum(square + 2.0 * rate * cross + rate * rate * grad_square, 0.0)
    shrink = jnp.minimum(1.0, radius_ref[plane] / jnp.sqrt(stepped_square + norm_epsilon))
    moved[...] = (current[...] + rate * gradient[...]) * shrink


def plane_plan(patch_embed, perturbation, target, ln_gain, ln_bias, w_qkv, w_out, radius, step_size):
    seq_count, planes = lax.axis_size("seq"), lax.axis_size("head")
    place, plane = lax.axis_index("seq"), lax.axis_index("head")
    chips = seq_count // 2
    chip, core = place // 2, place % 2
    _, part_rows, width = patch_embed.shape
    _, entries, _ = w_qkv.shape
    head_dim = entries // 3
    length = part_rows * seq_count
    half = length // 2
    embed, current, goal = patch_embed[0], perturbation[0], target[0]

    def swap(array, mask):
        return lax.ppermute(array, "seq", [(i, i ^ mask) for i in range(seq_count)])

    def device(chip, core, plane):
        return (chip * 2 + core) * planes + plane

    def hop(array, pairs):
        perm = [
            (device(c, *source), device(c, *dest)) for c in range(chips) for source, dest in pairs
        ]
        return lax.ppermute(array, ("seq", "head"), perm)

    def mirrored(pairs):
        flip = lambda end: (1 - end[0], planes - 1 - end[1])
        return pairs + [(flip(source), flip(dest)) for source, dest in pairs]

    first_hop = mirrored([((0, 1), (0, 0)), ((0, 0), (0, 1)), ((1, 1), (0, 2))])
    later_hops = [
        mirrored([((0, p), (0, p + 1)) for p in range(first, planes - 1)])
        for first in range(1, planes - 1)
    ]

    def chain(array):
        steps = [array, hop(array, first_hop)]
        for pairs in later_hops:
            steps.append(hop(steps[-1], pairs))
        return steps

    distance = jnp.where(core == 0, plane, planes - 1 - plane)
    depth = jnp.maximum(distance - 1, 0)

    shapes = [
        jax.ShapeDtypeStruct((rows, width), bf16)
        for rows in (part_rows, 2 * head_dim, 2 * head_dim)
    ]
    inputs = (embed, current, ln_gain, ln_bias)
    hidden, upper, lower = pl.pallas_call(
        begin_body,
        out_shape=shapes,
        in_specs=[SMEM] + [HBM] * 6,
        out_specs=[VMEM] * 3,
        scratch_shapes=[pltpu.VMEM(a.shape, a.dtype) for a in inputs]
        + [pltpu.SemaphoreType.DMA((7,))],
        compiler_params=pltpu.CompilerParams(vmem_limit_bytes=VMEM_LIMIT),
        name="begin",
    )(
        chip.reshape(1),
        *[pltpu.with_memory_space_constraint(a, pltpu.HBM) for a in (*inputs, w_qkv, w_out)],
    )
    lower_steps = chain(lower)
    upper_steps = chain(upper)
    masks = [2 * m + j for j in range(2) for m in range(chips)]

    def gather(array):
        same = [array] + [swap(array, 2 * m) for m in range(1, chips)]
        return same + [swap(part, 1) for part in same]

    def exchange(parts):
        return [parts[0]] + [swap(part, mask) for part, mask in zip(parts[1:], masks[1:])]

    hidden_rows = gather(hidden)

    def attend(uppers, lowers, earlier=()):
        square = length * length
        joined = [((2 * head_dim, part_rows), bf16)] * (seq_count if earlier else 0)
        return call(
            functools.partial(forward_body, seq_count, len(uppers), bool(earlier)),
            [
                ((entries, length), bf16),
                ((1, length), f32),
                ((entries, width), bf16),
                ((head_dim, length), bf16),
            ]
            + joined,
            depth.reshape(1),
            *uppers,
            *lowers,
            *hidden_rows,
            *earlier,
            scalars=1,
            flops=2 * length * entries * width + 4 * square * head_dim,
            exps=square,
        )

    near = attend(upper_steps[:-1], lower_steps[:-1])
    far = attend(upper_steps[1:], lower_steps[1:], near[3:4])
    slots = exchange(far[4:])
    (out_pair,) = call(
        pick_body, [((2 * head_dim, width), bf16)], depth.reshape(1), *lower_steps, scalars=1
    )
    weights = gather(out_pair)
    *grad_parts, residual = call(
        functools.partial(project_body, len(slots)),
        [((2 * head_dim, part_rows), bf16)] * seq_count + [((part_rows, width), f32)],
        embed,
        current,
        goal,
        *slots,
        *weights,
        flops=4 * part_rows * width * width,
    )
    arrived = exchange(grad_parts)
    grads, swapped = [], []
    for head, (packed, total, _, out, *_) in enumerate((near, far)):
        stay, leave = call(
            functools.partial(backward_body, head),
            [((entries, half), bf16)] * 2,
            packed,
            total,
            out,
            *arrived,
            flops=10 * length * length * head_dim,
            exps=length * length,
        )
        grads.append(stay)
        swapped.append(swap(leave, 1))
    both = [near[2], far[2]]
    others = [swap(w, 1) for w in both]
    own, *sent = call(
        functools.partial(hidden_grad_body, 4),
        [((part_rows, width), f32)] + [((part_rows, width), bf16)] * (chips - 1),
        *grads,
        *swapped,
        *both,
        *others,
        flops=8 * half * entries * width,
    )
    parts = [swap(part, 2 * (m + 1)) for m, part in enumerate(sent)]
    gradient, sums = call(
        gradient_body,
        [((part_rows, width), f32), ((8, 128), f32)],
        embed,
        current,
        residual,
        ln_gain,
        own,
        *parts,
    )
    sums = sums + swap(sums, 1)
    (moved,) = call(
        finish_body,
        [((part_rows, width), f32)],
        plane.reshape(1),
        step_size,
        radius,
        sums,
        *[swap(sums, 2 * m) for m in range(1, chips)],
        current,
        gradient,
        scalars=3,
    )
    return moved[None]


def on_device(patch_embed, perturbation, target, ln_gain, ln_bias, w_qkv, w_out, radius, step_size):
    seq_count, planes = lax.axis_size("seq"), lax.axis_size("head")
    own_images, part_rows, _ = patch_embed.shape
    local_heads, entries, _ = w_qkv.shape
    fits = (
        own_images == 1
        and 2 * local_heads == seq_count
        and seq_count == 8
        and planes == 4
        and part_rows % 128 == 0
        and entries % 48 == 0
    )
    plan = plane_plan if fits else general_plan
    return plan(
        patch_embed, perturbation, target, ln_gain, ln_bias, w_qkv, w_out, radius, step_size
    )


def solution(mesh):
    placed = (
        P("head", "seq", None),
        P("head", "seq", None),
        P("head", "seq", None),
        P(),
        P(),
        P("head", None, None),
        P("head", None, None),
        P(),
        P(),
    )
    return jax.shard_map(
        on_device, mesh=mesh, in_specs=placed, out_specs=P("head", "seq", None), check_vma=False
    )
```

```python
import functools
import math

import jax
import jax.numpy as jnp
from jax import lax
from jax.experimental import pallas as pl
from jax.experimental.pallas import tpu as pltpu
from jax.sharding import PartitionSpec as P

norm_epsilon = 1e-06
layer_epsilon = 1e-06


def layer_statistics(gathered):
    center = gathered - jnp.mean(gathered, axis=-1, keepdims=True)
    variance = jnp.mean(center * center, axis=-1, keepdims=True)
    inverse = lax.rsqrt(variance + layer_epsilon)
    return (center * inverse, inverse)


def attend_forward(queries, key_rows, values, score_scale):
    item_count, length, head_dim = queries.shape
    block_rows = min(512, length)
    query_blocks = queries.reshape(item_count, length // block_rows, block_rows, head_dim).swapaxes(
        0, 1
    )

    def one_block(query_block):
        scores = (
            jnp.einsum("nqe,nke->nqk", query_block, key_rows, preferred_element_type=jnp.float32)
            * score_scale
        )
        row_max = jnp.max(scores, axis=-1, keepdims=True)
        log_total = row_max + jnp.log(jnp.sum(jnp.exp(scores - row_max), axis=-1, keepdims=True))
        weights = jnp.exp(scores - log_total).astype(jnp.bfloat16)
        output = jnp.einsum(
            "nqk,nke->nqe", weights, values, preferred_element_type=jnp.float32
        ).astype(jnp.bfloat16)
        return (output, log_total[..., 0])

    output, log_total = lax.map(one_block, query_blocks)
    output = output.swapaxes(0, 1).reshape(item_count, length, head_dim)
    log_total = log_total.swapaxes(0, 1).reshape(item_count, length)
    return (output, log_total)


def attend_backward(queries, key_rows, values, output, log_total, grad_output, score_scale):
    item_count, length, head_dim = queries.shape
    block_rows = min(512, length)
    block_count = length // block_rows

    def cut_rows(array):
        return array.reshape((item_count, block_count, block_rows) + array.shape[2:]).swapaxes(0, 1)

    row_dot = jnp.sum(grad_output.astype(jnp.float32) * output.astype(jnp.float32), axis=-1)

    def one_block(carry, inputs):
        grad_keys, grad_values = carry
        query_block, grad_block, total_block, dot_block = inputs
        scores = (
            jnp.einsum("nqe,nke->nqk", query_block, key_rows, preferred_element_type=jnp.float32)
            * score_scale
        )
        weights = jnp.exp(scores - total_block[..., None])
        grad_values = grad_values + jnp.einsum(
            "nqk,nqe->nke",
            weights.astype(jnp.bfloat16),
            grad_block,
            preferred_element_type=jnp.float32,
        )
        grad_weights = jnp.einsum(
            "nqe,nke->nqk", grad_block, values, preferred_element_type=jnp.float32
        )
        grad_scores = (weights * (grad_weights - dot_block[..., None]) * score_scale).astype(
            jnp.bfloat16
        )
        grad_query = jnp.einsum(
            "nqk,nke->nqe", grad_scores, key_rows, preferred_element_type=jnp.float32
        ).astype(jnp.bfloat16)
        grad_keys = grad_keys + jnp.einsum(
            "nqk,nqe->nke", grad_scores, query_block, preferred_element_type=jnp.float32
        )
        return ((grad_keys, grad_values), grad_query)

    zero_rows = jnp.zeros((item_count, length, head_dim), jnp.float32)
    (grad_keys, grad_values), grad_query = lax.scan(
        one_block,
        (zero_rows, zero_rows),
        (cut_rows(queries), cut_rows(grad_output), cut_rows(log_total), cut_rows(row_dot)),
    )
    grad_query = grad_query.swapaxes(0, 1).reshape(item_count, length, head_dim)
    return jnp.concatenate(
        [grad_query, grad_keys.astype(jnp.bfloat16), grad_values.astype(jnp.bfloat16)], axis=-1
    )


def general_plan(patch_embed, perturbation, target, ln_gain, ln_bias, w_qkv, w_out, radius, step_size):
    seq_count = lax.axis_size("seq")
    own_images, part_rows, _ = patch_embed.shape
    local_heads = w_qkv.shape[0]
    head_dim = w_qkv.shape[1] // 3
    examples = own_images * lax.axis_size("head")
    pair_count = examples * local_heads // seq_count
    first_image = lax.axis_index("head") * own_images
    own_step = lax.dynamic_slice_in_dim(step_size, first_image, own_images, 0)
    own_radius = lax.dynamic_slice_in_dim(radius, first_image, own_images, 0)
    score_scale = 1.0 / math.sqrt(head_dim)
    current = perturbation
    mixed = patch_embed.astype(jnp.float32) + current
    rounded = mixed.astype(jnp.bfloat16)
    normed, inverse = layer_statistics(rounded.astype(jnp.float32))
    hidden = (normed * ln_gain + ln_bias).astype(jnp.bfloat16)
    hidden_all = lax.all_gather(hidden, "head", axis=0, tiled=True)
    packed = jnp.einsum(
        "epd,hcd->ehpc", hidden_all, w_qkv, preferred_element_type=jnp.float32
    ).astype(jnp.bfloat16)
    packed = packed.reshape(seq_count, pair_count, part_rows, 3 * head_dim)
    pair_rows = lax.all_to_all(packed, "seq", split_axis=0, concat_axis=2, tiled=True)[0]
    queries = pair_rows[..., :head_dim]
    key_rows = pair_rows[..., head_dim : 2 * head_dim]
    values = pair_rows[..., 2 * head_dim :]
    output, log_total = attend_forward(queries, key_rows, values, score_scale)
    returned = lax.all_to_all(output[None], "seq", split_axis=2, concat_axis=0, tiled=True)
    returned = returned.reshape(examples, local_heads, part_rows, head_dim)
    partial_value = jnp.einsum("ehpc,hcd->epd", returned, w_out, preferred_element_type=jnp.float32)
    branch = lax.psum_scatter(partial_value, "head", scatter_dimension=0, tiled=True)
    result = mixed + branch
    residual = result - target.astype(jnp.float32)
    residual_all = lax.all_gather(residual.astype(jnp.bfloat16), "head", axis=0, tiled=True)
    grad_output = jnp.einsum(
        "epd,hcd->ehpc", residual_all, w_out, preferred_element_type=jnp.float32
    ).astype(jnp.bfloat16)
    grad_output = grad_output.reshape(seq_count, pair_count, part_rows, head_dim)
    grad_pairs = lax.all_to_all(grad_output, "seq", split_axis=0, concat_axis=2, tiled=True)[0]
    grad_packed = attend_backward(
        queries, key_rows, values, output, log_total, grad_pairs, score_scale
    )
    grad_tokens = lax.all_to_all(grad_packed[None], "seq", split_axis=2, concat_axis=0, tiled=True)
    grad_tokens = grad_tokens.reshape(examples, local_heads, part_rows, 3 * head_dim)
    grad_partial = jnp.einsum(
        "ehpc,hcd->epd", grad_tokens, w_qkv, preferred_element_type=jnp.float32
    )
    grad_hidden = lax.psum_scatter(grad_partial, "head", scatter_dimension=0, tiled=True)
    scaled = grad_hidden * ln_gain
    first_mean = jnp.mean(scaled, axis=-1, keepdims=True)
    second_mean = jnp.mean(scaled * normed, axis=-1, keepdims=True)
    grad_input = (scaled - first_mean - normed * second_mean) * inverse
    gradient = residual + grad_input
    grad_square = lax.psum(jnp.sum(gradient * gradient, axis=(1, 2)), "seq")
    stepped = current + (own_step / jnp.sqrt(grad_square + norm_epsilon))[:, None, None] * gradient
    stepped_square = lax.psum(jnp.sum(stepped * stepped, axis=(1, 2)), "seq")
    current = (
        stepped
        * jnp.minimum(1.0, own_radius / jnp.sqrt(stepped_square + norm_epsilon))[:, None, None]
    )
    return current


LOG2E = math.log2(math.e)
bf16 = jnp.bfloat16
f32 = jnp.float32
VMEM = pl.BlockSpec(memory_space=pltpu.VMEM)
SMEM = pl.BlockSpec(memory_space=pltpu.SMEM)
HBM = pl.BlockSpec(memory_space=pltpu.HBM)
VMEM_LIMIT = 24 << 20


def dot(a, b, a_dim, b_dim):
    return lax.dot_general(a, b, (((a_dim,), (b_dim,)), ((), ())), preferred_element_type=f32)


def call(body, outs, *args, scalars=(), flops=0, exps=0):
    shapes = [jax.ShapeDtypeStruct(shape, dtype) for shape, dtype in outs]
    moved = sum(a.size * a.dtype.itemsize for a in list(args) + shapes)
    return pl.pallas_call(
        body,
        out_shape=shapes,
        in_specs=[SMEM if i in scalars else VMEM for i in range(len(args))],
        out_specs=[VMEM] * len(shapes),
        cost_estimate=pl.CostEstimate(flops=flops, transcendentals=exps, bytes_accessed=moved),
        compiler_params=pltpu.CompilerParams(vmem_limit_bytes=VMEM_LIMIT),
    )(*args)


def norm_parts(embed, current):
    rounded = (embed.astype(f32) + current).astype(bf16).astype(f32)
    center = rounded - jnp.mean(rounded, axis=-1, keepdims=True)
    inverse = lax.rsqrt(jnp.mean(center * center, axis=-1, keepdims=True) + layer_epsilon)
    return center * inverse, inverse


def begin_body(chip_ref, depth_ref, embed, current, gain, bias, qkv, out, hidden, upper, lower, *scratch):
    del depth_ref
    *held, sems = scratch
    chip = chip_ref[0]
    head_dim = out.shape[1]
    pairs = list(zip((embed, current, gain, bias), held))
    pairs += [
        (qkv.at[chip, pl.ds(0, 2 * head_dim)], upper),
        (qkv.at[chip, pl.ds(2 * head_dim, head_dim)], lower.at[pl.ds(0, head_dim)]),
        (out.at[chip], lower.at[pl.ds(head_dim, head_dim)]),
    ]
    copies = [
        pltpu.make_async_copy(source, dest, sems.at[i]) for i, (source, dest) in enumerate(pairs)
    ]
    for copy in copies:
        copy.start()
    for copy in copies[:4]:
        copy.wait()
    embed, current, gain, bias = held
    normed, _ = norm_parts(embed[...], current[...])
    hidden[...] = (normed * gain[...][None] + bias[...][None]).astype(bf16)
    for copy in copies[4:]:
        copy.wait()


def pick(depth, steps, cut):
    value = steps[0][cut, :]
    for i in range(1, len(steps)):
        value = jnp.where(depth == i, steps[i][cut, :], value)
    return value


def pick_body(depth_ref, *refs):
    steps, chosen = refs[:-1], refs[-1]
    size = chosen.shape[0]
    chosen[...] = pick(depth_ref[0], steps, slice(size, 2 * size))


def packed_body(places, choices, depth_ref, *refs):
    uppers, lowers, refs = refs[:choices], refs[choices : 2 * choices], refs[2 * choices :]
    hidden, (packed_ref, weight_ref) = refs[:places], refs[places:]
    depth = depth_ref[0]
    entries, _ = weight_ref.shape
    head_dim = entries // 3
    weight_ref[: 2 * head_dim, :] = pick(depth, uppers, slice(0, 2 * head_dim))
    weight_ref[2 * head_dim :, :] = pick(depth, lowers, slice(0, head_dim))
    rows = hidden[0].shape[0]
    for i in range(0, places, 2):
        rhs = jnp.concatenate([hidden[i][...], hidden[i + 1][...]], axis=0)
        packed_ref[:, i * rows : (i + 2) * rows] = dot(weight_ref[...], rhs, 1, 1).astype(bf16)


def attend(packed_ref, total_ref, out_ref):
    entries, length = packed_ref.shape
    head_dim = entries // 3
    scale = LOG2E / math.sqrt(head_dim)
    keys = packed_ref[head_dim : 2 * head_dim, :].T
    values_t = packed_ref[2 * head_dim :, :]
    step = min(256, length)
    for q in range(0, length, step):
        queries_t = packed_ref[:head_dim, q : q + step]
        scores = dot(keys, queries_t, 1, 0) * scale
        top = jnp.max(scores, axis=0, keepdims=True)
        raised = jnp.exp2(scores - top)
        total = jnp.sum(raised, axis=0, keepdims=True)
        total_ref[:, q : q + step] = top + jnp.log2(total)
        out = (dot(values_t, raised.astype(bf16), 1, 0) * (1.0 / total)).astype(bf16)
        out_ref[:, q : q + step] = out


def near_body(packed_ref, total_ref, out_ref):
    attend(packed_ref, total_ref, out_ref)


def far_body(places, choices, near_out, *refs):
    *inputs, packed_ref, weight_ref, total_ref, out_ref, same_ref, other_ref = refs
    packed_body(places, choices, *inputs, packed_ref, weight_ref)
    attend(packed_ref, total_ref, out_ref)
    chips, size, rows = same_ref.shape
    for i, dest in enumerate((same_ref, other_ref)):
        for m in range(chips):
            cut = slice((i * chips + m) * rows, (i * chips + m + 1) * rows)
            dest[m, : size // 2, :] = near_out[:, cut]
            dest[m, size // 2 :, :] = out_ref[:, cut]


def project_body(slots, embed, current, target, *refs):
    outs, weights = refs[:slots], refs[slots:-3]
    *grad_refs, residual_ref = refs[-3:]
    outs_t = jnp.concatenate([o[j] for j in range(len(grad_refs)) for o in outs], axis=0)
    full = jnp.concatenate([w[...] for w in weights], axis=0)
    branch = dot(outs_t, full, 0, 0)
    residual = embed[...].astype(f32) + current[...] + branch - target[...].astype(f32)
    residual_ref[...] = residual
    grads = dot(full, residual.astype(bf16), 1, 1).astype(bf16)
    size = grad_refs[0].shape[1]
    for i, dest in enumerate(grad_refs):
        for m in range(slots):
            start = (i * slots + m) * size
            dest[m] = grads[start : start + size, :]


def backward_body(head, packed_ref, total_ref, out_ref, *refs):
    arrived, (same_grad, other_grad) = refs[:-2], refs[-2:]
    entries, length = packed_ref.shape
    head_dim = entries // 3
    scale = 1.0 / math.sqrt(head_dim)
    cut = slice(head * head_dim, (head + 1) * head_dim)
    grads_t = jnp.concatenate([part[j, cut, :] for j in range(2) for part in arrived], axis=1)
    out_t = out_ref[...]
    queries_t = packed_ref[:head_dim, :]
    keys_t = packed_ref[head_dim : 2 * head_dim, :]
    keys = keys_t.T
    values = packed_ref[2 * head_dim :, :].T
    row_dot = jnp.sum(grads_t.astype(f32) * out_t.astype(f32), axis=0, keepdims=True)
    step = min(256, length)
    grad_keys = jnp.zeros((head_dim, length), f32)
    grad_values = jnp.zeros((head_dim, length), f32)
    half = length // 2
    for q in range(0, length, step):
        cut = slice(q, q + step)
        scores = dot(keys, queries_t[:, cut], 1, 0) * (scale * LOG2E)
        weights = jnp.exp2(scores - total_ref[:, cut])
        grad_weights = dot(values, grads_t[:, cut], 1, 0)
        grad_scores = (weights * (grad_weights - row_dot[:, cut]) * scale).astype(bf16)
        grad_values = grad_values + dot(grads_t[:, cut], weights.astype(bf16), 1, 1)
        grad_keys = grad_keys + dot(queries_t[:, cut], grad_scores, 1, 1)
        grad_query = dot(keys_t, grad_scores, 1, 0).astype(bf16)
        dest = same_grad if q < half else other_grad
        dest[:head_dim, q % half : q % half + step] = grad_query
    for i, dest in enumerate((same_grad, other_grad)):
        dest[head_dim : 2 * head_dim, :] = grad_keys[:, i * half : (i + 1) * half].astype(bf16)
        dest[2 * head_dim :, :] = grad_values[:, i * half : (i + 1) * half].astype(bf16)


def partial_body(*refs):
    count = len(refs) // 2
    refs[-1][...] = sum(dot(g[...], w[...], 0, 0) for g, w in zip(refs[:count], refs[count:-1]))


def hidden_grad_body(grad, weight, partial, own, *sent):
    rows = own.shape[0]
    total = partial[...] + dot(grad[...], weight[...], 0, 0)
    own[...] = total[:rows]
    for i, dest in enumerate(sent):
        dest[...] = total[(i + 1) * rows : (i + 2) * rows].astype(bf16)


def gradient_body(embed, current, residual, gain, own, *refs):
    arrived, (gradient_ref, sums_ref) = refs[:-2], refs[-2:]
    grad_hidden = own[...]
    for part in arrived:
        grad_hidden = grad_hidden + part[...].astype(f32)
    normed, inverse = norm_parts(embed[...], current[...])
    scaled = grad_hidden * gain[...][None]
    first_mean = jnp.mean(scaled, axis=-1, keepdims=True)
    second_mean = jnp.mean(scaled * normed, axis=-1, keepdims=True)
    gradient = residual[...] + (scaled - first_mean - normed * second_mean) * inverse
    gradient_ref[...] = gradient
    before = current[...]
    lanes = sums_ref.shape[1]
    sums_ref[...] = jnp.zeros_like(sums_ref)
    for i, terms in enumerate((gradient * gradient, before * gradient, before * before)):
        columns = jnp.sum(terms, axis=0, keepdims=True)
        sums_ref[i : i + 1, :] = sum(
            columns[:, j : j + lanes] for j in range(0, columns.shape[1], lanes)
        )


def finish_body(plane_ref, step_ref, radius_ref, *refs):
    *sum_refs, current, gradient, moved = refs
    sums = jnp.sum(sum(ref[...] for ref in sum_refs), axis=1, keepdims=True)
    grad_square, cross, square = sums[0:1], sums[1:2], sums[2:3]
    plane = plane_ref[0]
    rate = step_ref[plane] / jnp.sqrt(grad_square + norm_epsilon)
    stepped_square = jnp.maximum(square + 2.0 * rate * cross + rate * rate * grad_square, 0.0)
    shrink = jnp.minimum(1.0, radius_ref[plane] / jnp.sqrt(stepped_square + norm_epsilon))
    moved[...] = (current[...] + rate * gradient[...]) * shrink


def plane_plan(patch_embed, perturbation, target, ln_gain, ln_bias, w_qkv, w_out, radius, step_size):
    seq_count, planes = lax.axis_size("seq"), lax.axis_size("head")
    place, plane = lax.axis_index("seq"), lax.axis_index("head")
    chips = seq_count // 2
    chip, core = place // 2, place % 2
    _, part_rows, width = patch_embed.shape
    _, entries, _ = w_qkv.shape
    head_dim = entries // 3
    length = part_rows * seq_count
    half = length // 2
    embed, current, goal = patch_embed[0], perturbation[0], target[0]

    def swap(array, mask):
        return lax.ppermute(array, "seq", [(i, i ^ mask) for i in range(seq_count)])

    def device(chip, core, plane):
        return (chip * 2 + core) * planes + plane

    def hop(array, pairs):
        perm = [
            (device(c, *source), device(c, *dest)) for c in range(chips) for source, dest in pairs
        ]
        return lax.ppermute(array, ("seq", "head"), perm)

    def mirrored(pairs):
        flip = lambda end: (1 - end[0], planes - 1 - end[1])
        return pairs + [(flip(source), flip(dest)) for source, dest in pairs]

    first_hop = mirrored([((0, 1), (0, 0)), ((0, 0), (0, 1)), ((1, 1), (0, 2))])
    later_hops = [
        mirrored([((0, p), (0, p + 1)) for p in range(first, planes - 1)])
        for first in range(1, planes - 1)
    ]

    def chain(array):
        steps = [array, hop(array, first_hop)]
        for pairs in later_hops:
            steps.append(hop(steps[-1], pairs))
        return steps

    distance = jnp.where(core == 0, plane, planes - 1 - plane)
    depth = jnp.maximum(distance - 1, 0)

    shapes = [
        jax.ShapeDtypeStruct((rows, width), bf16)
        for rows in (part_rows, 2 * head_dim, 2 * head_dim)
    ]
    inputs = (embed, current, ln_gain, ln_bias)
    hidden, upper, lower = pl.pallas_call(
        begin_body,
        out_shape=shapes,
        in_specs=[SMEM] * 2 + [HBM] * 6,
        out_specs=[VMEM] * 3,
        scratch_shapes=[pltpu.VMEM(a.shape, a.dtype) for a in inputs]
        + [pltpu.SemaphoreType.DMA((7,))],
        compiler_params=pltpu.CompilerParams(vmem_limit_bytes=VMEM_LIMIT),
        name="bg",
    )(
        chip.reshape(1),
        depth.reshape(1),
        *[pltpu.with_memory_space_constraint(a, pltpu.HBM) for a in (*inputs, w_qkv, w_out)],
    )
    lower_steps = chain(lower)
    upper_steps = chain(upper)

    def gather(array):
        same = [array] + [swap(array, 2 * m) for m in range(1, chips)]
        return same + [swap(part, 1) for part in same]

    def exchange(same, other):
        arrived = swap(other, 1)
        pairs = [jnp.stack([same[m], arrived[m]]) for m in range(chips)]
        return [pairs[0]] + [swap(pairs[m], 2 * m) for m in range(1, chips)]

    hidden_rows = gather(hidden)

    square = length * length
    packed_outs = [((entries, length), bf16), ((entries, width), bf16)]
    attend_outs = [((1, length), f32), ((head_dim, length), bf16)]
    joined_outs = [((chips, 2 * head_dim, part_rows), bf16)] * 2
    pack_flops = 2 * length * entries * width
    near_packed, near_weight = call(
        functools.partial(packed_body, seq_count, planes - 1),
        packed_outs,
        depth.reshape(1),
        *upper_steps[:-1],
        *lower_steps[:-1],
        *hidden_rows,
        scalars=(0,),
        flops=pack_flops,
    )
    near_total, near_out = call(
        near_body, attend_outs, near_packed, flops=4 * square * head_dim, exps=square
    )
    far_packed, far_weight, far_total, far_out, *both_out = call(
        functools.partial(far_body, seq_count, planes - 1),
        packed_outs + attend_outs + joined_outs,
        near_out,
        depth.reshape(1),
        *upper_steps[1:],
        *lower_steps[1:],
        *hidden_rows,
        scalars=(1,),
        flops=pack_flops + 4 * square * head_dim,
        exps=square,
    )
    slots = exchange(*both_out)
    weights = []
    for lowers in (lower_steps[:-1], lower_steps[1:]):
        (own_rows,) = call(
            pick_body, [((head_dim, width), bf16)], depth.reshape(1), *lowers, scalars=(0,)
        )
        weights.append(gather(own_rows))
    weights = [part for pair in zip(*weights) for part in pair]
    *grad_parts, residual = call(
        functools.partial(project_body, len(slots)),
        [((chips, 2 * head_dim, part_rows), bf16)] * 2 + [((part_rows, width), f32)],
        embed,
        current,
        goal,
        *slots,
        *weights,
        flops=4 * part_rows * width * width,
    )
    arrived = exchange(*grad_parts)
    grads, swapped = [], []
    heads = (near_packed, near_total, near_out), (far_packed, far_total, far_out)
    for head, (packed, total, out) in enumerate(heads):
        stay, leave = call(
            functools.partial(backward_body, head),
            [((entries, half), bf16)] * 2,
            packed,
            total,
            out,
            *arrived,
            flops=10 * length * length * head_dim,
            exps=length * length,
        )
        grads.append(stay)
        swapped.append(swap(leave, 1))
    both = [near_weight, far_weight]
    others = [swap(w, 1) for w in both]
    (partial,) = call(
        partial_body,
        [((half, width), f32)],
        *grads,
        swapped[0],
        *both,
        others[0],
        flops=6 * half * entries * width,
    )
    own, *sent = call(
        hidden_grad_body,
        [((part_rows, width), f32)] + [((part_rows, width), bf16)] * (chips - 1),
        swapped[1],
        others[1],
        partial,
        flops=2 * half * entries * width,
    )
    parts = [swap(part, 2 * (m + 1)) for m, part in enumerate(sent)]
    gradient, sums = call(
        gradient_body,
        [((part_rows, width), f32), ((8, 128), f32)],
        embed,
        current,
        residual,
        ln_gain,
        own,
        *parts,
    )
    sums = sums + swap(sums, 1)
    (moved,) = call(
        finish_body,
        [((part_rows, width), f32)],
        plane.reshape(1),
        step_size,
        radius,
        sums,
        *[swap(sums, 2 * m) for m in range(1, chips)],
        current,
        gradient,
        scalars=(0, 1, 2),
    )
    return moved[None]


def on_device(patch_embed, perturbation, target, ln_gain, ln_bias, w_qkv, w_out, radius, step_size):
    seq_count, planes = lax.axis_size("seq"), lax.axis_size("head")
    own_images, part_rows, _ = patch_embed.shape
    local_heads, entries, _ = w_qkv.shape
    fits = (
        own_images == 1
        and 2 * local_heads == seq_count
        and seq_count == 8
        and planes == 4
        and part_rows % 128 == 0
        and entries % 48 == 0
    )
    plan = plane_plan if fits else general_plan
    return plan(
        patch_embed, perturbation, target, ln_gain, ln_bias, w_qkv, w_out, radius, step_size
    )


def solution(mesh):
    placed = (
        P("head", "seq", None),
        P("head", "seq", None),
        P("head", "seq", None),
        P(),
        P(),
        P("head", None, None),
        P("head", None, None),
        P(),
        P(),
    )
    return jax.shard_map(
        on_device, mesh=mesh, in_specs=placed, out_specs=P("head", "seq", None), check_vma=False
    )
```

```python
import functools
import math

import jax
import jax.numpy as jnp
from jax import lax
from jax.experimental import pallas as pl
from jax.experimental.pallas import tpu as pltpu
from jax.sharding import PartitionSpec as P

norm_epsilon = 1e-06
layer_epsilon = 1e-06


def layer_statistics(gathered):
    center = gathered - jnp.mean(gathered, axis=-1, keepdims=True)
    variance = jnp.mean(center * center, axis=-1, keepdims=True)
    inverse = lax.rsqrt(variance + layer_epsilon)
    return (center * inverse, inverse)


def attend_forward(queries, key_rows, values, score_scale):
    item_count, length, head_dim = queries.shape
    block_rows = min(512, length)
    query_blocks = queries.reshape(item_count, length // block_rows, block_rows, head_dim).swapaxes(
        0, 1
    )

    def one_block(query_block):
        scores = (
            jnp.einsum("nqe,nke->nqk", query_block, key_rows, preferred_element_type=jnp.float32)
            * score_scale
        )
        row_max = jnp.max(scores, axis=-1, keepdims=True)
        log_total = row_max + jnp.log(jnp.sum(jnp.exp(scores - row_max), axis=-1, keepdims=True))
        weights = jnp.exp(scores - log_total).astype(jnp.bfloat16)
        output = jnp.einsum(
            "nqk,nke->nqe", weights, values, preferred_element_type=jnp.float32
        ).astype(jnp.bfloat16)
        return (output, log_total[..., 0])

    output, log_total = lax.map(one_block, query_blocks)
    output = output.swapaxes(0, 1).reshape(item_count, length, head_dim)
    log_total = log_total.swapaxes(0, 1).reshape(item_count, length)
    return (output, log_total)


def attend_backward(queries, key_rows, values, output, log_total, grad_output, score_scale):
    item_count, length, head_dim = queries.shape
    block_rows = min(512, length)
    block_count = length // block_rows

    def cut_rows(array):
        return array.reshape((item_count, block_count, block_rows) + array.shape[2:]).swapaxes(0, 1)

    row_dot = jnp.sum(grad_output.astype(jnp.float32) * output.astype(jnp.float32), axis=-1)

    def one_block(carry, inputs):
        grad_keys, grad_values = carry
        query_block, grad_block, total_block, dot_block = inputs
        scores = (
            jnp.einsum("nqe,nke->nqk", query_block, key_rows, preferred_element_type=jnp.float32)
            * score_scale
        )
        weights = jnp.exp(scores - total_block[..., None])
        grad_values = grad_values + jnp.einsum(
            "nqk,nqe->nke",
            weights.astype(jnp.bfloat16),
            grad_block,
            preferred_element_type=jnp.float32,
        )
        grad_weights = jnp.einsum(
            "nqe,nke->nqk", grad_block, values, preferred_element_type=jnp.float32
        )
        grad_scores = (weights * (grad_weights - dot_block[..., None]) * score_scale).astype(
            jnp.bfloat16
        )
        grad_query = jnp.einsum(
            "nqk,nke->nqe", grad_scores, key_rows, preferred_element_type=jnp.float32
        ).astype(jnp.bfloat16)
        grad_keys = grad_keys + jnp.einsum(
            "nqk,nqe->nke", grad_scores, query_block, preferred_element_type=jnp.float32
        )
        return ((grad_keys, grad_values), grad_query)

    zero_rows = jnp.zeros((item_count, length, head_dim), jnp.float32)
    (grad_keys, grad_values), grad_query = lax.scan(
        one_block,
        (zero_rows, zero_rows),
        (cut_rows(queries), cut_rows(grad_output), cut_rows(log_total), cut_rows(row_dot)),
    )
    grad_query = grad_query.swapaxes(0, 1).reshape(item_count, length, head_dim)
    return jnp.concatenate(
        [grad_query, grad_keys.astype(jnp.bfloat16), grad_values.astype(jnp.bfloat16)], axis=-1
    )


def general_plan(patch_embed, perturbation, target, ln_gain, ln_bias, w_qkv, w_out, radius, step_size):
    seq_count = lax.axis_size("seq")
    own_images, part_rows, _ = patch_embed.shape
    local_heads = w_qkv.shape[0]
    head_dim = w_qkv.shape[1] // 3
    examples = own_images * lax.axis_size("head")
    pair_count = examples * local_heads // seq_count
    first_image = lax.axis_index("head") * own_images
    own_step = lax.dynamic_slice_in_dim(step_size, first_image, own_images, 0)
    own_radius = lax.dynamic_slice_in_dim(radius, first_image, own_images, 0)
    score_scale = 1.0 / math.sqrt(head_dim)
    current = perturbation
    mixed = patch_embed.astype(jnp.float32) + current
    rounded = mixed.astype(jnp.bfloat16)
    normed, inverse = layer_statistics(rounded.astype(jnp.float32))
    hidden = (normed * ln_gain + ln_bias).astype(jnp.bfloat16)
    hidden_all = lax.all_gather(hidden, "head", axis=0, tiled=True)
    packed = jnp.einsum(
        "epd,hcd->ehpc", hidden_all, w_qkv, preferred_element_type=jnp.float32
    ).astype(jnp.bfloat16)
    packed = packed.reshape(seq_count, pair_count, part_rows, 3 * head_dim)
    pair_rows = lax.all_to_all(packed, "seq", split_axis=0, concat_axis=2, tiled=True)[0]
    queries = pair_rows[..., :head_dim]
    key_rows = pair_rows[..., head_dim : 2 * head_dim]
    values = pair_rows[..., 2 * head_dim :]
    output, log_total = attend_forward(queries, key_rows, values, score_scale)
    returned = lax.all_to_all(output[None], "seq", split_axis=2, concat_axis=0, tiled=True)
    returned = returned.reshape(examples, local_heads, part_rows, head_dim)
    partial_value = jnp.einsum("ehpc,hcd->epd", returned, w_out, preferred_element_type=jnp.float32)
    branch = lax.psum_scatter(partial_value, "head", scatter_dimension=0, tiled=True)
    result = mixed + branch
    residual = result - target.astype(jnp.float32)
    residual_all = lax.all_gather(residual.astype(jnp.bfloat16), "head", axis=0, tiled=True)
    grad_output = jnp.einsum(
        "epd,hcd->ehpc", residual_all, w_out, preferred_element_type=jnp.float32
    ).astype(jnp.bfloat16)
    grad_output = grad_output.reshape(seq_count, pair_count, part_rows, head_dim)
    grad_pairs = lax.all_to_all(grad_output, "seq", split_axis=0, concat_axis=2, tiled=True)[0]
    grad_packed = attend_backward(
        queries, key_rows, values, output, log_total, grad_pairs, score_scale
    )
    grad_tokens = lax.all_to_all(grad_packed[None], "seq", split_axis=2, concat_axis=0, tiled=True)
    grad_tokens = grad_tokens.reshape(examples, local_heads, part_rows, 3 * head_dim)
    grad_partial = jnp.einsum(
        "ehpc,hcd->epd", grad_tokens, w_qkv, preferred_element_type=jnp.float32
    )
    grad_hidden = lax.psum_scatter(grad_partial, "head", scatter_dimension=0, tiled=True)
    scaled = grad_hidden * ln_gain
    first_mean = jnp.mean(scaled, axis=-1, keepdims=True)
    second_mean = jnp.mean(scaled * normed, axis=-1, keepdims=True)
    grad_input = (scaled - first_mean - normed * second_mean) * inverse
    gradient = residual + grad_input
    grad_square = lax.psum(jnp.sum(gradient * gradient, axis=(1, 2)), "seq")
    stepped = current + (own_step / jnp.sqrt(grad_square + norm_epsilon))[:, None, None] * gradient
    stepped_square = lax.psum(jnp.sum(stepped * stepped, axis=(1, 2)), "seq")
    current = (
        stepped
        * jnp.minimum(1.0, own_radius / jnp.sqrt(stepped_square + norm_epsilon))[:, None, None]
    )
    return current


LOG2E = math.log2(math.e)
bf16 = jnp.bfloat16
f32 = jnp.float32
VMEM = pl.BlockSpec(memory_space=pltpu.VMEM)
SMEM = pl.BlockSpec(memory_space=pltpu.SMEM)
HBM = pl.BlockSpec(memory_space=pltpu.HBM)
VMEM_LIMIT = 24 << 20


def dot(a, b, a_dim, b_dim):
    return lax.dot_general(a, b, (((a_dim,), (b_dim,)), ((), ())), preferred_element_type=f32)


def call(body, outs, *args, scalars=(), flops=0, exps=0):
    shapes = [jax.ShapeDtypeStruct(shape, dtype) for shape, dtype in outs]
    moved = sum(a.size * a.dtype.itemsize for a in list(args) + shapes)
    return pl.pallas_call(
        body,
        out_shape=shapes,
        in_specs=[SMEM if i in scalars else VMEM for i in range(len(args))],
        out_specs=[VMEM] * len(shapes),
        cost_estimate=pl.CostEstimate(flops=flops, transcendentals=exps, bytes_accessed=moved),
        compiler_params=pltpu.CompilerParams(vmem_limit_bytes=VMEM_LIMIT),
    )(*args)


def norm_parts(embed, current):
    rounded = (embed.astype(f32) + current).astype(bf16).astype(f32)
    center = rounded - jnp.mean(rounded, axis=-1, keepdims=True)
    inverse = lax.rsqrt(jnp.mean(center * center, axis=-1, keepdims=True) + layer_epsilon)
    return center * inverse, inverse


def begin_body(chip_ref, depth_ref, embed, current, gain, bias, qkv, out, hidden, upper, lower, *scratch):
    del depth_ref
    *held, sems = scratch
    chip = chip_ref[0]
    head_dim = out.shape[1]
    pairs = list(zip((embed, current, gain, bias), held))
    pairs += [
        (qkv.at[chip, pl.ds(0, 2 * head_dim)], upper),
        (qkv.at[chip, pl.ds(2 * head_dim, head_dim)], lower.at[pl.ds(0, head_dim)]),
        (out.at[chip], lower.at[pl.ds(head_dim, head_dim)]),
    ]
    copies = [
        pltpu.make_async_copy(source, dest, sems.at[i]) for i, (source, dest) in enumerate(pairs)
    ]
    for copy in copies:
        copy.start()
    for copy in copies[:4]:
        copy.wait()
    embed, current, gain, bias = held
    normed, _ = norm_parts(embed[...], current[...])
    hidden[...] = (normed * gain[...][None] + bias[...][None]).astype(bf16)
    for copy in copies[4:]:
        copy.wait()


def pick(depth, steps, cut):
    value = steps[0][cut, :]
    for i in range(1, len(steps)):
        value = jnp.where(depth == i, steps[i][cut, :], value)
    return value


def pick_body(depth_ref, *refs):
    steps, chosen = refs[:-1], refs[-1]
    size = chosen.shape[0]
    chosen[...] = pick(depth_ref[0], steps, slice(size, 2 * size))


def packed_body(places, choices, depth_ref, *refs):
    uppers, lowers, refs = refs[:choices], refs[choices : 2 * choices], refs[2 * choices :]
    hidden, (packed_ref, weight_ref) = refs[:places], refs[places:]
    depth = depth_ref[0]
    entries, _ = weight_ref.shape
    head_dim = entries // 3
    weight_ref[: 2 * head_dim, :] = pick(depth, uppers, slice(0, 2 * head_dim))
    weight_ref[2 * head_dim :, :] = pick(depth, lowers, slice(0, head_dim))
    rows = hidden[0].shape[0]
    for i in range(0, places, 2):
        rhs = jnp.concatenate([hidden[i][...], hidden[i + 1][...]], axis=0)
        packed_ref[:, i * rows : (i + 2) * rows] = dot(weight_ref[...], rhs, 1, 1).astype(bf16)


def attend(packed_ref, total_ref, out_ref):
    entries, _ = packed_ref.shape
    head_dim = entries // 3
    scale = LOG2E / math.sqrt(head_dim)
    keys = packed_ref[head_dim : 2 * head_dim, :].T
    values_t = packed_ref[2 * head_dim :, :]
    scores = dot(keys, packed_ref[:head_dim, :], 1, 0) * scale
    top = jnp.max(scores, axis=0, keepdims=True)
    raised = jnp.exp2(scores - top)
    total = jnp.sum(raised, axis=0, keepdims=True)
    total_ref[...] = top + jnp.log2(total)
    out_ref[...] = (dot(values_t, raised.astype(bf16), 1, 0) * (1.0 / total)).astype(bf16)


def near_body(packed_ref, total_ref, out_ref):
    attend(packed_ref, total_ref, out_ref)


def far_body(places, choices, near_out, *refs):
    *inputs, packed_ref, weight_ref, total_ref, out_ref, same_ref, other_ref = refs
    packed_body(places, choices, *inputs, packed_ref, weight_ref)
    attend(packed_ref, total_ref, out_ref)
    chips, size, rows = same_ref.shape
    for i, dest in enumerate((same_ref, other_ref)):
        for m in range(chips):
            cut = slice((i * chips + m) * rows, (i * chips + m + 1) * rows)
            dest[m, : size // 2, :] = near_out[:, cut]
            dest[m, size // 2 :, :] = out_ref[:, cut]


def project_body(slots, embed, current, target, *refs):
    outs, weights = refs[:slots], refs[slots:-3]
    *grad_refs, residual_ref = refs[-3:]
    outs_t = jnp.concatenate([o[j] for j in range(len(grad_refs)) for o in outs], axis=0)
    full = jnp.concatenate([w[...] for w in weights], axis=0)
    branch = dot(outs_t, full, 0, 0)
    residual = embed[...].astype(f32) + current[...] + branch - target[...].astype(f32)
    residual_ref[...] = residual
    grads = dot(full, residual.astype(bf16), 1, 1).astype(bf16)
    size = grad_refs[0].shape[1]
    for i, dest in enumerate(grad_refs):
        for m in range(slots):
            start = (i * slots + m) * size
            dest[m] = grads[start : start + size, :]


def backward_body(head, packed_ref, total_ref, out_ref, *refs):
    arrived, (same_grad, other_grad) = refs[:-2], refs[-2:]
    entries, length = packed_ref.shape
    head_dim = entries // 3
    scale = 1.0 / math.sqrt(head_dim)
    cut = slice(head * head_dim, (head + 1) * head_dim)
    grads_t = jnp.concatenate([part[j, cut, :] for j in range(2) for part in arrived], axis=1)
    out_t = out_ref[...]
    queries_t = packed_ref[:head_dim, :]
    keys_t = packed_ref[head_dim : 2 * head_dim, :]
    keys = keys_t.T
    values = packed_ref[2 * head_dim :, :].T
    row_dot = jnp.sum(grads_t.astype(f32) * out_t.astype(f32), axis=0, keepdims=True)
    step = min(512, length)
    grad_keys = jnp.zeros((head_dim, length), f32)
    grad_values = jnp.zeros((head_dim, length), f32)
    half = length // 2
    for q in range(0, length, step):
        cut = slice(q, q + step)
        scores = dot(keys, queries_t[:, cut], 1, 0) * (scale * LOG2E)
        weights = jnp.exp2(scores - total_ref[:, cut])
        grad_weights = dot(values, grads_t[:, cut], 1, 0)
        grad_scores = (weights * (grad_weights - row_dot[:, cut]) * scale).astype(bf16)
        grad_values = grad_values + dot(grads_t[:, cut], weights.astype(bf16), 1, 1)
        grad_keys = grad_keys + dot(queries_t[:, cut], grad_scores, 1, 1)
        grad_query = dot(keys_t, grad_scores, 1, 0).astype(bf16)
        dest = same_grad if q < half else other_grad
        dest[:head_dim, q % half : q % half + step] = grad_query
    for i, dest in enumerate((same_grad, other_grad)):
        dest[head_dim : 2 * head_dim, :] = grad_keys[:, i * half : (i + 1) * half].astype(bf16)
        dest[2 * head_dim :, :] = grad_values[:, i * half : (i + 1) * half].astype(bf16)


def partial_body(*refs):
    count = len(refs) // 2
    refs[-1][...] = sum(dot(g[...], w[...], 0, 0) for g, w in zip(refs[:count], refs[count:-1]))


def hidden_grad_body(grad, weight, partial, own, *sent):
    rows = own.shape[0]
    total = partial[...] + dot(grad[...], weight[...], 0, 0)
    own[...] = total[:rows]
    for i, dest in enumerate(sent):
        dest[...] = total[(i + 1) * rows : (i + 2) * rows].astype(bf16)


def gradient_body(embed, current, residual, gain, own, *refs):
    arrived, (gradient_ref, sums_ref) = refs[:-2], refs[-2:]
    grad_hidden = own[...]
    for part in arrived:
        grad_hidden = grad_hidden + part[...].astype(f32)
    normed, inverse = norm_parts(embed[...], current[...])
    scaled = grad_hidden * gain[...][None]
    first_mean = jnp.mean(scaled, axis=-1, keepdims=True)
    second_mean = jnp.mean(scaled * normed, axis=-1, keepdims=True)
    gradient = residual[...] + (scaled - first_mean - normed * second_mean) * inverse
    gradient_ref[...] = gradient
    before = current[...]
    lanes = sums_ref.shape[1]
    sums_ref[...] = jnp.zeros_like(sums_ref)
    for i, terms in enumerate((gradient * gradient, before * gradient, before * before)):
        columns = jnp.sum(terms, axis=0, keepdims=True)
        sums_ref[i : i + 1, :] = sum(
            columns[:, j : j + lanes] for j in range(0, columns.shape[1], lanes)
        )


def finish_body(plane_ref, step_ref, radius_ref, *refs):
    *sum_refs, current, gradient, moved = refs
    sums = jnp.sum(sum(ref[...] for ref in sum_refs), axis=1, keepdims=True)
    grad_square, cross, square = sums[0:1], sums[1:2], sums[2:3]
    plane = plane_ref[0]
    rate = step_ref[plane] / jnp.sqrt(grad_square + norm_epsilon)
    stepped_square = jnp.maximum(square + 2.0 * rate * cross + rate * rate * grad_square, 0.0)
    shrink = jnp.minimum(1.0, radius_ref[plane] / jnp.sqrt(stepped_square + norm_epsilon))
    moved[...] = (current[...] + rate * gradient[...]) * shrink


def plane_plan(patch_embed, perturbation, target, ln_gain, ln_bias, w_qkv, w_out, radius, step_size):
    seq_count, planes = lax.axis_size("seq"), lax.axis_size("head")
    place, plane = lax.axis_index("seq"), lax.axis_index("head")
    chips = seq_count // 2
    chip, core = place // 2, place % 2
    _, part_rows, width = patch_embed.shape
    _, entries, _ = w_qkv.shape
    head_dim = entries // 3
    length = part_rows * seq_count
    half = length // 2
    embed, current, goal = patch_embed[0], perturbation[0], target[0]

    def swap(array, mask):
        return lax.ppermute(array, "seq", [(i, i ^ mask) for i in range(seq_count)])

    def device(chip, core, plane):
        return (chip * 2 + core) * planes + plane

    def hop(array, pairs):
        perm = [
            (device(c, *source), device(c, *dest)) for c in range(chips) for source, dest in pairs
        ]
        return lax.ppermute(array, ("seq", "head"), perm)

    def mirrored(pairs):
        flip = lambda end: (1 - end[0], planes - 1 - end[1])
        return pairs + [(flip(source), flip(dest)) for source, dest in pairs]

    first_hop = mirrored([((0, 1), (0, 0)), ((0, 0), (0, 1)), ((1, 1), (0, 2))])
    later_hops = [
        mirrored([((0, p), (0, p + 1)) for p in range(first, planes - 1)])
        for first in range(1, planes - 1)
    ]

    def chain(array):
        steps = [array, hop(array, first_hop)]
        for pairs in later_hops:
            steps.append(hop(steps[-1], pairs))
        return steps

    distance = jnp.where(core == 0, plane, planes - 1 - plane)
    depth = jnp.maximum(distance - 1, 0)

    shapes = [
        jax.ShapeDtypeStruct((rows, width), bf16)
        for rows in (part_rows, 2 * head_dim, 2 * head_dim)
    ]
    inputs = (embed, current, ln_gain, ln_bias)
    hidden, upper, lower = pl.pallas_call(
        begin_body,
        out_shape=shapes,
        in_specs=[SMEM] * 2 + [HBM] * 6,
        out_specs=[VMEM] * 3,
        scratch_shapes=[pltpu.VMEM(a.shape, a.dtype) for a in inputs]
        + [pltpu.SemaphoreType.DMA((7,))],
        compiler_params=pltpu.CompilerParams(vmem_limit_bytes=VMEM_LIMIT),
        name="bg",
    )(
        chip.reshape(1),
        depth.reshape(1),
        *[pltpu.with_memory_space_constraint(a, pltpu.HBM) for a in (*inputs, w_qkv, w_out)],
    )
    lower_steps = chain(lower)
    upper_steps = chain(upper)

    def gather(array):
        same = [array] + [swap(array, 2 * m) for m in range(1, chips)]
        return same + [swap(part, 1) for part in same]

    def exchange(same, other):
        arrived = swap(other, 1)
        pairs = [jnp.stack([same[m], arrived[m]]) for m in range(chips)]
        return [pairs[0]] + [swap(pairs[m], 2 * m) for m in range(1, chips)]

    hidden_rows = gather(hidden)

    square = length * length
    packed_outs = [((entries, length), bf16), ((entries, width), bf16)]
    attend_outs = [((1, length), f32), ((head_dim, length), bf16)]
    joined_outs = [((chips, 2 * head_dim, part_rows), bf16)] * 2
    pack_flops = 2 * length * entries * width
    near_packed, near_weight = call(
        functools.partial(packed_body, seq_count, planes - 1),
        packed_outs,
        depth.reshape(1),
        *upper_steps[:-1],
        *lower_steps[:-1],
        *hidden_rows,
        scalars=(0,),
        flops=pack_flops,
    )
    near_total, near_out = call(
        near_body, attend_outs, near_packed, flops=4 * square * head_dim, exps=square
    )
    far_packed, far_weight, far_total, far_out, *both_out = call(
        functools.partial(far_body, seq_count, planes - 1),
        packed_outs + attend_outs + joined_outs,
        near_out,
        depth.reshape(1),
        *upper_steps[1:],
        *lower_steps[1:],
        *hidden_rows,
        scalars=(1,),
        flops=pack_flops + 4 * square * head_dim,
        exps=square,
    )
    slots = exchange(*both_out)
    weights = []
    for lowers in (lower_steps[:-1], lower_steps[1:]):
        (own_rows,) = call(
            pick_body, [((head_dim, width), bf16)], depth.reshape(1), *lowers, scalars=(0,)
        )
        weights.append(gather(own_rows))
    weights = [part for pair in zip(*weights) for part in pair]
    *grad_parts, residual = call(
        functools.partial(project_body, len(slots)),
        [((chips, 2 * head_dim, part_rows), bf16)] * 2 + [((part_rows, width), f32)],
        embed,
        current,
        goal,
        *slots,
        *weights,
        flops=4 * part_rows * width * width,
    )
    arrived = exchange(*grad_parts)
    grads, swapped = [], []
    heads = (near_packed, near_total, near_out), (far_packed, far_total, far_out)
    for head, (packed, total, out) in enumerate(heads):
        stay, leave = call(
            functools.partial(backward_body, head),
            [((entries, half), bf16)] * 2,
            packed,
            total,
            out,
            *arrived,
            flops=10 * length * length * head_dim,
            exps=length * length,
        )
        grads.append(stay)
        swapped.append(swap(leave, 1))
    both = [near_weight, far_weight]
    others = [swap(w, 1) for w in both]
    (partial,) = call(
        partial_body,
        [((half, width), f32)],
        *grads,
        swapped[0],
        *both,
        others[0],
        flops=6 * half * entries * width,
    )
    own, *sent = call(
        hidden_grad_body,
        [((part_rows, width), f32)] + [((part_rows, width), bf16)] * (chips - 1),
        swapped[1],
        others[1],
        partial,
        flops=2 * half * entries * width,
    )
    parts = [swap(part, 2 * (m + 1)) for m, part in enumerate(sent)]
    gradient, sums = call(
        gradient_body,
        [((part_rows, width), f32), ((8, 128), f32)],
        embed,
        current,
        residual,
        ln_gain,
        own,
        *parts,
    )
    sums = sums + swap(sums, 1)
    (moved,) = call(
        finish_body,
        [((part_rows, width), f32)],
        plane.reshape(1),
        step_size,
        radius,
        sums,
        *[swap(sums, 2 * m) for m in range(1, chips)],
        current,
        gradient,
        scalars=(0, 1, 2),
    )
    return moved[None]


def on_device(patch_embed, perturbation, target, ln_gain, ln_bias, w_qkv, w_out, radius, step_size):
    seq_count, planes = lax.axis_size("seq"), lax.axis_size("head")
    own_images, part_rows, _ = patch_embed.shape
    local_heads, entries, _ = w_qkv.shape
    fits = (
        own_images == 1
        and 2 * local_heads == seq_count
        and seq_count == 8
        and planes == 4
        and part_rows % 128 == 0
        and entries % 48 == 0
    )
    plan = plane_plan if fits else general_plan
    return plan(
        patch_embed, perturbation, target, ln_gain, ln_bias, w_qkv, w_out, radius, step_size
    )


def solution(mesh):
    placed = (
        P("head", "seq", None),
        P("head", "seq", None),
        P("head", "seq", None),
        P(),
        P(),
        P("head", None, None),
        P("head", None, None),
        P(),
        P(),
    )
    return jax.shard_map(
        on_device, mesh=mesh, in_specs=placed, out_specs=P("head", "seq", None), check_vma=False
    )
```

```python
import functools
import math

import jax
import jax.numpy as jnp
from jax import lax
from jax.experimental import pallas as pl
from jax.experimental.pallas import tpu as pltpu
from jax.sharding import PartitionSpec as P

norm_epsilon = 1e-06
layer_epsilon = 1e-06


def layer_statistics(gathered):
    center = gathered - jnp.mean(gathered, axis=-1, keepdims=True)
    variance = jnp.mean(center * center, axis=-1, keepdims=True)
    inverse = lax.rsqrt(variance + layer_epsilon)
    return (center * inverse, inverse)


def attend_forward(queries, key_rows, values, score_scale):
    item_count, length, head_dim = queries.shape
    block_rows = min(512, length)
    query_blocks = queries.reshape(item_count, length // block_rows, block_rows, head_dim).swapaxes(
        0, 1
    )

    def one_block(query_block):
        scores = (
            jnp.einsum("nqe,nke->nqk", query_block, key_rows, preferred_element_type=jnp.float32)
            * score_scale
        )
        row_max = jnp.max(scores, axis=-1, keepdims=True)
        log_total = row_max + jnp.log(jnp.sum(jnp.exp(scores - row_max), axis=-1, keepdims=True))
        weights = jnp.exp(scores - log_total).astype(jnp.bfloat16)
        output = jnp.einsum(
            "nqk,nke->nqe", weights, values, preferred_element_type=jnp.float32
        ).astype(jnp.bfloat16)
        return (output, log_total[..., 0])

    output, log_total = lax.map(one_block, query_blocks)
    output = output.swapaxes(0, 1).reshape(item_count, length, head_dim)
    log_total = log_total.swapaxes(0, 1).reshape(item_count, length)
    return (output, log_total)


def attend_backward(queries, key_rows, values, output, log_total, grad_output, score_scale):
    item_count, length, head_dim = queries.shape
    block_rows = min(512, length)
    block_count = length // block_rows

    def cut_rows(array):
        return array.reshape((item_count, block_count, block_rows) + array.shape[2:]).swapaxes(0, 1)

    row_dot = jnp.sum(grad_output.astype(jnp.float32) * output.astype(jnp.float32), axis=-1)

    def one_block(carry, inputs):
        grad_keys, grad_values = carry
        query_block, grad_block, total_block, dot_block = inputs
        scores = (
            jnp.einsum("nqe,nke->nqk", query_block, key_rows, preferred_element_type=jnp.float32)
            * score_scale
        )
        weights = jnp.exp(scores - total_block[..., None])
        grad_values = grad_values + jnp.einsum(
            "nqk,nqe->nke",
            weights.astype(jnp.bfloat16),
            grad_block,
            preferred_element_type=jnp.float32,
        )
        grad_weights = jnp.einsum(
            "nqe,nke->nqk", grad_block, values, preferred_element_type=jnp.float32
        )
        grad_scores = (weights * (grad_weights - dot_block[..., None]) * score_scale).astype(
            jnp.bfloat16
        )
        grad_query = jnp.einsum(
            "nqk,nke->nqe", grad_scores, key_rows, preferred_element_type=jnp.float32
        ).astype(jnp.bfloat16)
        grad_keys = grad_keys + jnp.einsum(
            "nqk,nqe->nke", grad_scores, query_block, preferred_element_type=jnp.float32
        )
        return ((grad_keys, grad_values), grad_query)

    zero_rows = jnp.zeros((item_count, length, head_dim), jnp.float32)
    (grad_keys, grad_values), grad_query = lax.scan(
        one_block,
        (zero_rows, zero_rows),
        (cut_rows(queries), cut_rows(grad_output), cut_rows(log_total), cut_rows(row_dot)),
    )
    grad_query = grad_query.swapaxes(0, 1).reshape(item_count, length, head_dim)
    return jnp.concatenate(
        [grad_query, grad_keys.astype(jnp.bfloat16), grad_values.astype(jnp.bfloat16)], axis=-1
    )


def general_plan(patch_embed, perturbation, target, ln_gain, ln_bias, w_qkv, w_out, radius, step_size):
    seq_count = lax.axis_size("seq")
    own_images, part_rows, _ = patch_embed.shape
    local_heads = w_qkv.shape[0]
    head_dim = w_qkv.shape[1] // 3
    examples = own_images * lax.axis_size("head")
    pair_count = examples * local_heads // seq_count
    first_image = lax.axis_index("head") * own_images
    own_step = lax.dynamic_slice_in_dim(step_size, first_image, own_images, 0)
    own_radius = lax.dynamic_slice_in_dim(radius, first_image, own_images, 0)
    score_scale = 1.0 / math.sqrt(head_dim)
    current = perturbation
    mixed = patch_embed.astype(jnp.float32) + current
    rounded = mixed.astype(jnp.bfloat16)
    normed, inverse = layer_statistics(rounded.astype(jnp.float32))
    hidden = (normed * ln_gain + ln_bias).astype(jnp.bfloat16)
    hidden_all = lax.all_gather(hidden, "head", axis=0, tiled=True)
    packed = jnp.einsum(
        "epd,hcd->ehpc", hidden_all, w_qkv, preferred_element_type=jnp.float32
    ).astype(jnp.bfloat16)
    packed = packed.reshape(seq_count, pair_count, part_rows, 3 * head_dim)
    pair_rows = lax.all_to_all(packed, "seq", split_axis=0, concat_axis=2, tiled=True)[0]
    queries = pair_rows[..., :head_dim]
    key_rows = pair_rows[..., head_dim : 2 * head_dim]
    values = pair_rows[..., 2 * head_dim :]
    output, log_total = attend_forward(queries, key_rows, values, score_scale)
    returned = lax.all_to_all(output[None], "seq", split_axis=2, concat_axis=0, tiled=True)
    returned = returned.reshape(examples, local_heads, part_rows, head_dim)
    partial_value = jnp.einsum("ehpc,hcd->epd", returned, w_out, preferred_element_type=jnp.float32)
    branch = lax.psum_scatter(partial_value, "head", scatter_dimension=0, tiled=True)
    result = mixed + branch
    residual = result - target.astype(jnp.float32)
    residual_all = lax.all_gather(residual.astype(jnp.bfloat16), "head", axis=0, tiled=True)
    grad_output = jnp.einsum(
        "epd,hcd->ehpc", residual_all, w_out, preferred_element_type=jnp.float32
    ).astype(jnp.bfloat16)
    grad_output = grad_output.reshape(seq_count, pair_count, part_rows, head_dim)
    grad_pairs = lax.all_to_all(grad_output, "seq", split_axis=0, concat_axis=2, tiled=True)[0]
    grad_packed = attend_backward(
        queries, key_rows, values, output, log_total, grad_pairs, score_scale
    )
    grad_tokens = lax.all_to_all(grad_packed[None], "seq", split_axis=2, concat_axis=0, tiled=True)
    grad_tokens = grad_tokens.reshape(examples, local_heads, part_rows, 3 * head_dim)
    grad_partial = jnp.einsum(
        "ehpc,hcd->epd", grad_tokens, w_qkv, preferred_element_type=jnp.float32
    )
    grad_hidden = lax.psum_scatter(grad_partial, "head", scatter_dimension=0, tiled=True)
    scaled = grad_hidden * ln_gain
    first_mean = jnp.mean(scaled, axis=-1, keepdims=True)
    second_mean = jnp.mean(scaled * normed, axis=-1, keepdims=True)
    grad_input = (scaled - first_mean - normed * second_mean) * inverse
    gradient = residual + grad_input
    grad_square = lax.psum(jnp.sum(gradient * gradient, axis=(1, 2)), "seq")
    stepped = current + (own_step / jnp.sqrt(grad_square + norm_epsilon))[:, None, None] * gradient
    stepped_square = lax.psum(jnp.sum(stepped * stepped, axis=(1, 2)), "seq")
    current = (
        stepped
        * jnp.minimum(1.0, own_radius / jnp.sqrt(stepped_square + norm_epsilon))[:, None, None]
    )
    return current


LOG2E = math.log2(math.e)
bf16 = jnp.bfloat16
f32 = jnp.float32
VMEM = pl.BlockSpec(memory_space=pltpu.VMEM)
SMEM = pl.BlockSpec(memory_space=pltpu.SMEM)
HBM = pl.BlockSpec(memory_space=pltpu.HBM)
VMEM_LIMIT = 24 << 20


def dot(a, b, a_dim, b_dim):
    return lax.dot_general(a, b, (((a_dim,), (b_dim,)), ((), ())), preferred_element_type=f32)


def call(body, outs, *args, scalars=(), flops=0, exps=0):
    shapes = [jax.ShapeDtypeStruct(shape, dtype) for shape, dtype in outs]
    moved = sum(a.size * a.dtype.itemsize for a in list(args) + shapes)
    return pl.pallas_call(
        body,
        out_shape=shapes,
        in_specs=[SMEM if i in scalars else VMEM for i in range(len(args))],
        out_specs=[VMEM] * len(shapes),
        cost_estimate=pl.CostEstimate(flops=flops, transcendentals=exps, bytes_accessed=moved),
        compiler_params=pltpu.CompilerParams(vmem_limit_bytes=VMEM_LIMIT),
    )(*args)


def norm_parts(embed, current):
    rounded = (embed.astype(f32) + current).astype(bf16).astype(f32)
    center = rounded - jnp.mean(rounded, axis=-1, keepdims=True)
    inverse = lax.rsqrt(jnp.mean(center * center, axis=-1, keepdims=True) + layer_epsilon)
    return center * inverse, inverse


def begin_body(chip_ref, depth_ref, embed, current, gain, bias, qkv, out, hidden, upper, lower, *scratch):
    del depth_ref
    *held, sems = scratch
    chip = chip_ref[0]
    head_dim = out.shape[1]
    pairs = list(zip((embed, current, gain, bias), held))
    pairs += [
        (qkv.at[chip, pl.ds(0, 2 * head_dim)], upper),
        (qkv.at[chip, pl.ds(2 * head_dim, head_dim)], lower.at[pl.ds(0, head_dim)]),
        (out.at[chip], lower.at[pl.ds(head_dim, head_dim)]),
    ]
    copies = [
        pltpu.make_async_copy(source, dest, sems.at[i]) for i, (source, dest) in enumerate(pairs)
    ]
    for copy in copies:
        copy.start()
    for copy in copies[:4]:
        copy.wait()
    embed, current, gain, bias = held
    normed, _ = norm_parts(embed[...], current[...])
    hidden[...] = (normed * gain[...][None] + bias[...][None]).astype(bf16)
    for copy in copies[4:]:
        copy.wait()


def pick(depth, steps, cut):
    value = steps[0][cut, :]
    for i in range(1, len(steps)):
        value = jnp.where(depth == i, steps[i][cut, :], value)
    return value


def pick_body(depth_ref, *refs):
    steps, chosen = refs[:-1], refs[-1]
    size = chosen.shape[0]
    chosen[...] = pick(depth_ref[0], steps, slice(size, 2 * size))


def packed_body(places, choices, depth_ref, *refs):
    uppers, lowers, refs = refs[:choices], refs[choices : 2 * choices], refs[2 * choices :]
    hidden, (packed_ref, weight_ref) = refs[:places], refs[places:]
    depth = depth_ref[0]
    entries, _ = weight_ref.shape
    head_dim = entries // 3
    weight_ref[: 2 * head_dim, :] = pick(depth, uppers, slice(0, 2 * head_dim))
    weight_ref[2 * head_dim :, :] = pick(depth, lowers, slice(0, head_dim))
    rows = hidden[0].shape[0]
    for i in range(0, places, 2):
        rhs = jnp.concatenate([hidden[i][...], hidden[i + 1][...]], axis=0)
        packed_ref[:, i * rows : (i + 2) * rows] = dot(weight_ref[...], rhs, 1, 1).astype(bf16)


def attend(packed_ref, kept_ref, out_ref):
    entries, _ = packed_ref.shape
    head_dim = entries // 3
    scale = LOG2E / math.sqrt(head_dim)
    keys = packed_ref[head_dim : 2 * head_dim, :].T
    values_t = packed_ref[2 * head_dim :, :]
    scores = dot(keys, packed_ref[:head_dim, :], 1, 0) * scale
    top = jnp.max(scores, axis=0, keepdims=True)
    raised = jnp.exp2(scores - top)
    total = jnp.sum(raised, axis=0, keepdims=True)
    weights = (raised * (1.0 / total)).astype(bf16)
    kept_ref[...] = weights
    out_ref[...] = dot(values_t, weights, 1, 0).astype(bf16)


def near_body(packed_ref, kept_ref, out_ref):
    attend(packed_ref, kept_ref, out_ref)


def far_body(places, choices, near_out, *refs):
    *inputs, packed_ref, weight_ref, kept_ref, out_ref, same_ref, other_ref = refs
    packed_body(places, choices, *inputs, packed_ref, weight_ref)
    attend(packed_ref, kept_ref, out_ref)
    chips, size, rows = same_ref.shape
    for i, dest in enumerate((same_ref, other_ref)):
        for m in range(chips):
            cut = slice((i * chips + m) * rows, (i * chips + m + 1) * rows)
            dest[m, : size // 2, :] = near_out[:, cut]
            dest[m, size // 2 :, :] = out_ref[:, cut]


def project_body(slots, embed, current, target, *refs):
    outs, weights = refs[:slots], refs[slots:-3]
    *grad_refs, residual_ref = refs[-3:]
    outs_t = jnp.concatenate([o[j] for j in range(len(grad_refs)) for o in outs], axis=0)
    full = jnp.concatenate([w[...] for w in weights], axis=0)
    branch = dot(outs_t, full, 0, 0)
    residual = embed[...].astype(f32) + current[...] + branch - target[...].astype(f32)
    residual_ref[...] = residual
    grads = dot(full, residual.astype(bf16), 1, 1).astype(bf16)
    size = grad_refs[0].shape[1]
    for i, dest in enumerate(grad_refs):
        for m in range(slots):
            start = (i * slots + m) * size
            dest[m] = grads[start : start + size, :]


def backward_body(head, packed_ref, kept_ref, out_ref, *refs):
    arrived, (same_grad, other_grad) = refs[:-2], refs[-2:]
    entries, length = packed_ref.shape
    head_dim = entries // 3
    scale = 1.0 / math.sqrt(head_dim)
    cut = slice(head * head_dim, (head + 1) * head_dim)
    grads_t = jnp.concatenate([part[j, cut, :] for j in range(2) for part in arrived], axis=1)
    out_t = out_ref[...]
    queries_t = packed_ref[:head_dim, :]
    keys_t = packed_ref[head_dim : 2 * head_dim, :]
    values = packed_ref[2 * head_dim :, :].T
    row_dot = jnp.sum(grads_t.astype(f32) * out_t.astype(f32), axis=0, keepdims=True)
    step = min(512, length)
    grad_keys = jnp.zeros((head_dim, length), f32)
    grad_values = jnp.zeros((head_dim, length), f32)
    half = length // 2
    for q in range(0, length, step):
        cut = slice(q, q + step)
        weights = kept_ref[:, cut]
        grad_weights = dot(values, grads_t[:, cut], 1, 0)
        grad_scores = weights.astype(f32) * (grad_weights - row_dot[:, cut])
        grad_scores = (grad_scores * scale).astype(bf16)
        grad_values = grad_values + dot(grads_t[:, cut], weights, 1, 1)
        grad_keys = grad_keys + dot(queries_t[:, cut], grad_scores, 1, 1)
        grad_query = dot(keys_t, grad_scores, 1, 0).astype(bf16)
        dest = same_grad if q < half else other_grad
        dest[:head_dim, q % half : q % half + step] = grad_query
    for i, dest in enumerate((same_grad, other_grad)):
        dest[head_dim : 2 * head_dim, :] = grad_keys[:, i * half : (i + 1) * half].astype(bf16)
        dest[2 * head_dim :, :] = grad_values[:, i * half : (i + 1) * half].astype(bf16)


def partial_body(*refs):
    count = len(refs) // 2
    refs[-1][...] = sum(dot(g[...], w[...], 0, 0) for g, w in zip(refs[:count], refs[count:-1]))


def hidden_grad_body(grad, weight, partial, own, *sent):
    rows = own.shape[0]
    total = partial[...] + dot(grad[...], weight[...], 0, 0)
    own[...] = total[:rows]
    for i, dest in enumerate(sent):
        dest[...] = total[(i + 1) * rows : (i + 2) * rows].astype(bf16)


def gradient_body(embed, current, residual, gain, own, *refs):
    arrived, (gradient_ref, sums_ref) = refs[:-2], refs[-2:]
    grad_hidden = own[...]
    for part in arrived:
        grad_hidden = grad_hidden + part[...].astype(f32)
    normed, inverse = norm_parts(embed[...], current[...])
    scaled = grad_hidden * gain[...][None]
    first_mean = jnp.mean(scaled, axis=-1, keepdims=True)
    second_mean = jnp.mean(scaled * normed, axis=-1, keepdims=True)
    gradient = residual[...] + (scaled - first_mean - normed * second_mean) * inverse
    gradient_ref[...] = gradient
    before = current[...]
    lanes = sums_ref.shape[1]
    sums_ref[...] = jnp.zeros_like(sums_ref)
    for i, terms in enumerate((gradient * gradient, before * gradient, before * before)):
        columns = jnp.sum(terms, axis=0, keepdims=True)
        sums_ref[i : i + 1, :] = sum(
            columns[:, j : j + lanes] for j in range(0, columns.shape[1], lanes)
        )


def finish_body(plane_ref, step_ref, radius_ref, *refs):
    *sum_refs, current, gradient, moved = refs
    sums = jnp.sum(sum(ref[...] for ref in sum_refs), axis=1, keepdims=True)
    grad_square, cross, square = sums[0:1], sums[1:2], sums[2:3]
    plane = plane_ref[0]
    rate = step_ref[plane] / jnp.sqrt(grad_square + norm_epsilon)
    stepped_square = jnp.maximum(square + 2.0 * rate * cross + rate * rate * grad_square, 0.0)
    shrink = jnp.minimum(1.0, radius_ref[plane] / jnp.sqrt(stepped_square + norm_epsilon))
    moved[...] = (current[...] + rate * gradient[...]) * shrink


def plane_plan(patch_embed, perturbation, target, ln_gain, ln_bias, w_qkv, w_out, radius, step_size):
    seq_count, planes = lax.axis_size("seq"), lax.axis_size("head")
    place, plane = lax.axis_index("seq"), lax.axis_index("head")
    chips = seq_count // 2
    chip, core = place // 2, place % 2
    _, part_rows, width = patch_embed.shape
    _, entries, _ = w_qkv.shape
    head_dim = entries // 3
    length = part_rows * seq_count
    half = length // 2
    embed, current, goal = patch_embed[0], perturbation[0], target[0]

    def swap(array, mask):
        return lax.ppermute(array, "seq", [(i, i ^ mask) for i in range(seq_count)])

    def device(chip, core, plane):
        return (chip * 2 + core) * planes + plane

    def hop(array, pairs):
        perm = [
            (device(c, *source), device(c, *dest)) for c in range(chips) for source, dest in pairs
        ]
        return lax.ppermute(array, ("seq", "head"), perm)

    def mirrored(pairs):
        flip = lambda end: (1 - end[0], planes - 1 - end[1])
        return pairs + [(flip(source), flip(dest)) for source, dest in pairs]

    first_hop = mirrored([((0, 1), (0, 0)), ((0, 0), (0, 1)), ((1, 1), (0, 2))])
    later_hops = [
        mirrored([((0, p), (0, p + 1)) for p in range(first, planes - 1)])
        for first in range(1, planes - 1)
    ]

    def chain(array):
        steps = [array, hop(array, first_hop)]
        for pairs in later_hops:
            steps.append(hop(steps[-1], pairs))
        return steps

    distance = jnp.where(core == 0, plane, planes - 1 - plane)
    depth = jnp.maximum(distance - 1, 0)

    shapes = [
        jax.ShapeDtypeStruct((rows, width), bf16)
        for rows in (part_rows, 2 * head_dim, 2 * head_dim)
    ]
    inputs = (embed, current, ln_gain, ln_bias)
    hidden, upper, lower = pl.pallas_call(
        begin_body,
        out_shape=shapes,
        in_specs=[SMEM] * 2 + [HBM] * 6,
        out_specs=[VMEM] * 3,
        scratch_shapes=[pltpu.VMEM(a.shape, a.dtype) for a in inputs]
        + [pltpu.SemaphoreType.DMA((7,))],
        compiler_params=pltpu.CompilerParams(vmem_limit_bytes=VMEM_LIMIT),
        name="bg",
    )(
        chip.reshape(1),
        depth.reshape(1),
        *[pltpu.with_memory_space_constraint(a, pltpu.HBM) for a in (*inputs, w_qkv, w_out)],
    )
    lower_steps = chain(lower)
    upper_steps = chain(upper)

    def gather(array):
        same = [array] + [swap(array, 2 * m) for m in range(1, chips)]
        return same + [swap(part, 1) for part in same]

    def exchange(same, other):
        arrived = swap(other, 1)
        pairs = [jnp.stack([same[m], arrived[m]]) for m in range(chips)]
        return [pairs[0]] + [swap(pairs[m], 2 * m) for m in range(1, chips)]

    hidden_rows = gather(hidden)

    square = length * length
    packed_outs = [((entries, length), bf16), ((entries, width), bf16)]
    attend_outs = [((length, length), bf16), ((head_dim, length), bf16)]
    joined_outs = [((chips, 2 * head_dim, part_rows), bf16)] * 2
    pack_flops = 2 * length * entries * width
    near_packed, near_weight = call(
        functools.partial(packed_body, seq_count, planes - 1),
        packed_outs,
        depth.reshape(1),
        *upper_steps[:-1],
        *lower_steps[:-1],
        *hidden_rows,
        scalars=(0,),
        flops=pack_flops,
    )
    near_kept, near_out = call(
        near_body, attend_outs, near_packed, flops=4 * square * head_dim, exps=square
    )
    far_packed, far_weight, far_kept, far_out, *both_out = call(
        functools.partial(far_body, seq_count, planes - 1),
        packed_outs + attend_outs + joined_outs,
        near_out,
        depth.reshape(1),
        *upper_steps[1:],
        *lower_steps[1:],
        *hidden_rows,
        scalars=(1,),
        flops=pack_flops + 4 * square * head_dim,
        exps=square,
    )
    slots = exchange(*both_out)
    weights = []
    for lowers in (lower_steps[:-1], lower_steps[1:]):
        (own_rows,) = call(
            pick_body, [((head_dim, width), bf16)], depth.reshape(1), *lowers, scalars=(0,)
        )
        weights.append(gather(own_rows))
    weights = [part for pair in zip(*weights) for part in pair]
    *grad_parts, residual = call(
        functools.partial(project_body, len(slots)),
        [((chips, 2 * head_dim, part_rows), bf16)] * 2 + [((part_rows, width), f32)],
        embed,
        current,
        goal,
        *slots,
        *weights,
        flops=4 * part_rows * width * width,
    )
    arrived = exchange(*grad_parts)
    grads, swapped = [], []
    heads = (near_packed, near_kept, near_out), (far_packed, far_kept, far_out)
    for head, (packed, kept, out) in enumerate(heads):
        stay, leave = call(
            functools.partial(backward_body, head),
            [((entries, half), bf16)] * 2,
            packed,
            kept,
            out,
            *arrived,
            flops=8 * length * length * head_dim,
        )
        grads.append(stay)
        swapped.append(swap(leave, 1))
    both = [near_weight, far_weight]
    others = [swap(w, 1) for w in both]
    (partial,) = call(
        partial_body,
        [((half, width), f32)],
        *grads,
        swapped[0],
        *both,
        others[0],
        flops=6 * half * entries * width,
    )
    own, *sent = call(
        hidden_grad_body,
        [((part_rows, width), f32)] + [((part_rows, width), bf16)] * (chips - 1),
        swapped[1],
        others[1],
        partial,
        flops=2 * half * entries * width,
    )
    parts = [swap(part, 2 * (m + 1)) for m, part in enumerate(sent)]
    gradient, sums = call(
        gradient_body,
        [((part_rows, width), f32), ((8, 128), f32)],
        embed,
        current,
        residual,
        ln_gain,
        own,
        *parts,
    )
    sums = sums + swap(sums, 1)
    (moved,) = call(
        finish_body,
        [((part_rows, width), f32)],
        plane.reshape(1),
        step_size,
        radius,
        sums,
        *[swap(sums, 2 * m) for m in range(1, chips)],
        current,
        gradient,
        scalars=(0, 1, 2),
    )
    return moved[None]


def on_device(patch_embed, perturbation, target, ln_gain, ln_bias, w_qkv, w_out, radius, step_size):
    seq_count, planes = lax.axis_size("seq"), lax.axis_size("head")
    own_images, part_rows, _ = patch_embed.shape
    local_heads, entries, _ = w_qkv.shape
    fits = (
        own_images == 1
        and 2 * local_heads == seq_count
        and seq_count == 8
        and planes == 4
        and part_rows % 128 == 0
        and entries % 48 == 0
    )
    plan = plane_plan if fits else general_plan
    return plan(
        patch_embed, perturbation, target, ln_gain, ln_bias, w_qkv, w_out, radius, step_size
    )


def solution(mesh):
    placed = (
        P("head", "seq", None),
        P("head", "seq", None),
        P("head", "seq", None),
        P(),
        P(),
        P("head", None, None),
        P("head", None, None),
        P(),
        P(),
    )
    return jax.shard_map(
        on_device, mesh=mesh, in_specs=placed, out_specs=P("head", "seq", None), check_vma=False
    )
```

```python
import functools
import math

import jax
import jax.numpy as jnp
from jax import lax
from jax.experimental import pallas as pl
from jax.experimental.pallas import tpu as pltpu
from jax.sharding import PartitionSpec as P

norm_epsilon = 1e-06
layer_epsilon = 1e-06


def layer_statistics(gathered):
    center = gathered - jnp.mean(gathered, axis=-1, keepdims=True)
    variance = jnp.mean(center * center, axis=-1, keepdims=True)
    inverse = lax.rsqrt(variance + layer_epsilon)
    return (center * inverse, inverse)


def attend_forward(queries, key_rows, values, score_scale):
    item_count, length, head_dim = queries.shape
    block_rows = min(512, length)
    query_blocks = queries.reshape(item_count, length // block_rows, block_rows, head_dim).swapaxes(
        0, 1
    )

    def one_block(query_block):
        scores = (
            jnp.einsum("nqe,nke->nqk", query_block, key_rows, preferred_element_type=jnp.float32)
            * score_scale
        )
        row_max = jnp.max(scores, axis=-1, keepdims=True)
        log_total = row_max + jnp.log(jnp.sum(jnp.exp(scores - row_max), axis=-1, keepdims=True))
        weights = jnp.exp(scores - log_total).astype(jnp.bfloat16)
        output = jnp.einsum(
            "nqk,nke->nqe", weights, values, preferred_element_type=jnp.float32
        ).astype(jnp.bfloat16)
        return (output, log_total[..., 0])

    output, log_total = lax.map(one_block, query_blocks)
    output = output.swapaxes(0, 1).reshape(item_count, length, head_dim)
    log_total = log_total.swapaxes(0, 1).reshape(item_count, length)
    return (output, log_total)


def attend_backward(queries, key_rows, values, output, log_total, grad_output, score_scale):
    item_count, length, head_dim = queries.shape
    block_rows = min(512, length)
    block_count = length // block_rows

    def cut_rows(array):
        return array.reshape((item_count, block_count, block_rows) + array.shape[2:]).swapaxes(0, 1)

    row_dot = jnp.sum(grad_output.astype(jnp.float32) * output.astype(jnp.float32), axis=-1)

    def one_block(carry, inputs):
        grad_keys, grad_values = carry
        query_block, grad_block, total_block, dot_block = inputs
        scores = (
            jnp.einsum("nqe,nke->nqk", query_block, key_rows, preferred_element_type=jnp.float32)
            * score_scale
        )
        weights = jnp.exp(scores - total_block[..., None])
        grad_values = grad_values + jnp.einsum(
            "nqk,nqe->nke",
            weights.astype(jnp.bfloat16),
            grad_block,
            preferred_element_type=jnp.float32,
        )
        grad_weights = jnp.einsum(
            "nqe,nke->nqk", grad_block, values, preferred_element_type=jnp.float32
        )
        grad_scores = (weights * (grad_weights - dot_block[..., None]) * score_scale).astype(
            jnp.bfloat16
        )
        grad_query = jnp.einsum(
            "nqk,nke->nqe", grad_scores, key_rows, preferred_element_type=jnp.float32
        ).astype(jnp.bfloat16)
        grad_keys = grad_keys + jnp.einsum(
            "nqk,nqe->nke", grad_scores, query_block, preferred_element_type=jnp.float32
        )
        return ((grad_keys, grad_values), grad_query)

    zero_rows = jnp.zeros((item_count, length, head_dim), jnp.float32)
    (grad_keys, grad_values), grad_query = lax.scan(
        one_block,
        (zero_rows, zero_rows),
        (cut_rows(queries), cut_rows(grad_output), cut_rows(log_total), cut_rows(row_dot)),
    )
    grad_query = grad_query.swapaxes(0, 1).reshape(item_count, length, head_dim)
    return jnp.concatenate(
        [grad_query, grad_keys.astype(jnp.bfloat16), grad_values.astype(jnp.bfloat16)], axis=-1
    )


def general_plan(patch_embed, perturbation, target, ln_gain, ln_bias, w_qkv, w_out, radius, step_size):
    seq_count = lax.axis_size("seq")
    own_images, part_rows, _ = patch_embed.shape
    local_heads = w_qkv.shape[0]
    head_dim = w_qkv.shape[1] // 3
    examples = own_images * lax.axis_size("head")
    pair_count = examples * local_heads // seq_count
    first_image = lax.axis_index("head") * own_images
    own_step = lax.dynamic_slice_in_dim(step_size, first_image, own_images, 0)
    own_radius = lax.dynamic_slice_in_dim(radius, first_image, own_images, 0)
    score_scale = 1.0 / math.sqrt(head_dim)
    current = perturbation
    mixed = patch_embed.astype(jnp.float32) + current
    rounded = mixed.astype(jnp.bfloat16)
    normed, inverse = layer_statistics(rounded.astype(jnp.float32))
    hidden = (normed * ln_gain + ln_bias).astype(jnp.bfloat16)
    hidden_all = lax.all_gather(hidden, "head", axis=0, tiled=True)
    packed = jnp.einsum(
        "epd,hcd->ehpc", hidden_all, w_qkv, preferred_element_type=jnp.float32
    ).astype(jnp.bfloat16)
    packed = packed.reshape(seq_count, pair_count, part_rows, 3 * head_dim)
    pair_rows = lax.all_to_all(packed, "seq", split_axis=0, concat_axis=2, tiled=True)[0]
    queries = pair_rows[..., :head_dim]
    key_rows = pair_rows[..., head_dim : 2 * head_dim]
    values = pair_rows[..., 2 * head_dim :]
    output, log_total = attend_forward(queries, key_rows, values, score_scale)
    returned = lax.all_to_all(output[None], "seq", split_axis=2, concat_axis=0, tiled=True)
    returned = returned.reshape(examples, local_heads, part_rows, head_dim)
    partial_value = jnp.einsum("ehpc,hcd->epd", returned, w_out, preferred_element_type=jnp.float32)
    branch = lax.psum_scatter(partial_value, "head", scatter_dimension=0, tiled=True)
    result = mixed + branch
    residual = result - target.astype(jnp.float32)
    residual_all = lax.all_gather(residual.astype(jnp.bfloat16), "head", axis=0, tiled=True)
    grad_output = jnp.einsum(
        "epd,hcd->ehpc", residual_all, w_out, preferred_element_type=jnp.float32
    ).astype(jnp.bfloat16)
    grad_output = grad_output.reshape(seq_count, pair_count, part_rows, head_dim)
    grad_pairs = lax.all_to_all(grad_output, "seq", split_axis=0, concat_axis=2, tiled=True)[0]
    grad_packed = attend_backward(
        queries, key_rows, values, output, log_total, grad_pairs, score_scale
    )
    grad_tokens = lax.all_to_all(grad_packed[None], "seq", split_axis=2, concat_axis=0, tiled=True)
    grad_tokens = grad_tokens.reshape(examples, local_heads, part_rows, 3 * head_dim)
    grad_partial = jnp.einsum(
        "ehpc,hcd->epd", grad_tokens, w_qkv, preferred_element_type=jnp.float32
    )
    grad_hidden = lax.psum_scatter(grad_partial, "head", scatter_dimension=0, tiled=True)
    scaled = grad_hidden * ln_gain
    first_mean = jnp.mean(scaled, axis=-1, keepdims=True)
    second_mean = jnp.mean(scaled * normed, axis=-1, keepdims=True)
    grad_input = (scaled - first_mean - normed * second_mean) * inverse
    gradient = residual + grad_input
    grad_square = lax.psum(jnp.sum(gradient * gradient, axis=(1, 2)), "seq")
    stepped = current + (own_step / jnp.sqrt(grad_square + norm_epsilon))[:, None, None] * gradient
    stepped_square = lax.psum(jnp.sum(stepped * stepped, axis=(1, 2)), "seq")
    current = (
        stepped
        * jnp.minimum(1.0, own_radius / jnp.sqrt(stepped_square + norm_epsilon))[:, None, None]
    )
    return current


LOG2E = math.log2(math.e)
bf16 = jnp.bfloat16
f32 = jnp.float32
VMEM = pl.BlockSpec(memory_space=pltpu.VMEM)
SMEM = pl.BlockSpec(memory_space=pltpu.SMEM)
HBM = pl.BlockSpec(memory_space=pltpu.HBM)
VMEM_LIMIT = 24 << 20


def dot(a, b, a_dim, b_dim):
    return lax.dot_general(a, b, (((a_dim,), (b_dim,)), ((), ())), preferred_element_type=f32)


def call(body, outs, *args, scalars=(), flops=0, exps=0):
    shapes = [jax.ShapeDtypeStruct(shape, dtype) for shape, dtype in outs]
    moved = sum(a.size * a.dtype.itemsize for a in list(args) + shapes)
    return pl.pallas_call(
        body,
        out_shape=shapes,
        in_specs=[SMEM if i in scalars else VMEM for i in range(len(args))],
        out_specs=[VMEM] * len(shapes),
        cost_estimate=pl.CostEstimate(flops=flops, transcendentals=exps, bytes_accessed=moved),
        compiler_params=pltpu.CompilerParams(vmem_limit_bytes=VMEM_LIMIT),
    )(*args)


def norm_parts(embed, current):
    rounded = (embed.astype(f32) + current).astype(bf16).astype(f32)
    center = rounded - jnp.mean(rounded, axis=-1, keepdims=True)
    inverse = lax.rsqrt(jnp.mean(center * center, axis=-1, keepdims=True) + layer_epsilon)
    return center * inverse, inverse


def begin_body(chip_ref, depth_ref, embed, current, gain, bias, qkv, out, hidden, upper, lower, *scratch):
    del depth_ref
    *held, sems = scratch
    chip = chip_ref[0]
    head_dim = out.shape[1]
    pairs = list(zip((embed, current, gain, bias), held))
    pairs += [
        (qkv.at[chip, pl.ds(0, 2 * head_dim)], upper),
        (qkv.at[chip, pl.ds(2 * head_dim, head_dim)], lower.at[pl.ds(0, head_dim)]),
        (out.at[chip], lower.at[pl.ds(head_dim, head_dim)]),
    ]
    copies = [
        pltpu.make_async_copy(source, dest, sems.at[i]) for i, (source, dest) in enumerate(pairs)
    ]
    for copy in copies:
        copy.start()
    for copy in copies[:4]:
        copy.wait()
    embed, current, gain, bias = held
    normed, _ = norm_parts(embed[...], current[...])
    hidden[...] = (normed * gain[...][None] + bias[...][None]).astype(bf16)
    for copy in copies[4:]:
        copy.wait()


def pick(depth, steps, cut):
    value = steps[0][cut, :]
    for i in range(1, len(steps)):
        value = jnp.where(depth == i, steps[i][cut, :], value)
    return value


def pick_body(depth_ref, *refs):
    steps, chosen = refs[:-1], refs[-1]
    size = chosen.shape[0]
    chosen[...] = pick(depth_ref[0], steps, slice(size, 2 * size))


def packed_body(places, choices, depth_ref, *refs):
    uppers, lowers, refs = refs[:choices], refs[choices : 2 * choices], refs[2 * choices :]
    hidden, (packed_ref, weight_ref) = refs[:places], refs[places:]
    depth = depth_ref[0]
    entries, _ = weight_ref.shape
    head_dim = entries // 3
    weight_ref[: 2 * head_dim, :] = pick(depth, uppers, slice(0, 2 * head_dim))
    weight_ref[2 * head_dim :, :] = pick(depth, lowers, slice(0, head_dim))
    rows = hidden[0].shape[0]
    for i in range(0, places, 2):
        rhs = jnp.concatenate([hidden[i][...], hidden[i + 1][...]], axis=0)
        packed_ref[:, i * rows : (i + 2) * rows] = dot(weight_ref[...], rhs, 1, 1).astype(bf16)


def attend(packed_ref, kept_ref, out_ref):
    entries, _ = packed_ref.shape
    head_dim = entries // 3
    scale = LOG2E / math.sqrt(head_dim)
    keys = packed_ref[head_dim : 2 * head_dim, :].T
    values_t = packed_ref[2 * head_dim :, :]
    scores = dot(keys, packed_ref[:head_dim, :], 1, 0) * scale
    top = jnp.max(scores, axis=0, keepdims=True)
    raised = jnp.exp2(scores - top)
    total = jnp.sum(raised, axis=0, keepdims=True)
    weights = (raised * (1.0 / total)).astype(bf16)
    kept_ref[...] = weights
    out_ref[...] = dot(values_t, weights, 1, 0).astype(bf16)


def near_body(packed_ref, kept_ref, out_ref):
    attend(packed_ref, kept_ref, out_ref)


def far_body(places, choices, near_out, *refs):
    *inputs, packed_ref, weight_ref, kept_ref, out_ref, same_ref, other_ref = refs
    packed_body(places, choices, *inputs, packed_ref, weight_ref)
    attend(packed_ref, kept_ref, out_ref)
    chips, size, rows = same_ref.shape
    for i, dest in enumerate((same_ref, other_ref)):
        for m in range(chips):
            cut = slice((i * chips + m) * rows, (i * chips + m + 1) * rows)
            dest[m, : size // 2, :] = near_out[:, cut]
            dest[m, size // 2 :, :] = out_ref[:, cut]


def project_body(slots, embed, current, target, *refs):
    outs, weights = refs[:slots], refs[slots:-3]
    *grad_refs, residual_ref = refs[-3:]
    outs_t = jnp.concatenate([o[j] for j in range(len(grad_refs)) for o in outs], axis=0)
    full = jnp.concatenate([w[...] for w in weights], axis=0)
    branch = dot(outs_t, full, 0, 0)
    residual = embed[...].astype(f32) + current[...] + branch - target[...].astype(f32)
    residual_ref[...] = residual
    grads = dot(full, residual.astype(bf16), 1, 1).astype(bf16)
    size = grad_refs[0].shape[1]
    for i, dest in enumerate(grad_refs):
        for m in range(slots):
            start = (i * slots + m) * size
            dest[m] = grads[start : start + size, :]


def backward_body(head, packed_ref, kept_ref, out_ref, *refs):
    arrived, (same_grad, other_grad) = refs[:-2], refs[-2:]
    entries, length = packed_ref.shape
    head_dim = entries // 3
    scale = 1.0 / math.sqrt(head_dim)
    cut = slice(head * head_dim, (head + 1) * head_dim)
    grads_t = jnp.concatenate([part[j, cut, :] for j in range(2) for part in arrived], axis=1)
    out_t = out_ref[...]
    queries_t = packed_ref[:head_dim, :]
    keys_t = packed_ref[head_dim : 2 * head_dim, :]
    values = packed_ref[2 * head_dim :, :].T
    row_dot = jnp.sum(grads_t.astype(f32) * out_t.astype(f32), axis=0, keepdims=True)
    step = min(512, length)
    grad_keys = jnp.zeros((head_dim, length), f32)
    grad_values = jnp.zeros((head_dim, length), f32)
    half = length // 2
    for q in range(0, length, step):
        cut = slice(q, q + step)
        weights = kept_ref[:, cut]
        grad_weights = dot(values, grads_t[:, cut], 1, 0)
        grad_scores = (weights.astype(f32) * (grad_weights - row_dot[:, cut])).astype(bf16)
        grad_values = grad_values + dot(grads_t[:, cut], weights, 1, 1)
        grad_keys = grad_keys + dot(queries_t[:, cut], grad_scores, 1, 1)
        grad_query = (dot(keys_t, grad_scores, 1, 0) * scale).astype(bf16)
        dest = same_grad if q < half else other_grad
        dest[:head_dim, q % half : q % half + step] = grad_query
    for i, dest in enumerate((same_grad, other_grad)):
        grad_part = grad_keys[:, i * half : (i + 1) * half] * scale
        dest[head_dim : 2 * head_dim, :] = grad_part.astype(bf16)
        dest[2 * head_dim :, :] = grad_values[:, i * half : (i + 1) * half].astype(bf16)


def partial_body(*refs):
    count = len(refs) // 2
    refs[-1][...] = sum(dot(g[...], w[...], 0, 0) for g, w in zip(refs[:count], refs[count:-1]))


def hidden_grad_body(grad, weight, partial, own, *sent):
    rows = own.shape[0]
    total = partial[...] + dot(grad[...], weight[...], 0, 0)
    own[...] = total[:rows]
    for i, dest in enumerate(sent):
        dest[...] = total[(i + 1) * rows : (i + 2) * rows].astype(bf16)


def gradient_body(embed, current, residual, gain, own, *refs):
    arrived, (gradient_ref, sums_ref) = refs[:-2], refs[-2:]
    grad_hidden = own[...]
    for part in arrived:
        grad_hidden = grad_hidden + part[...].astype(f32)
    normed, inverse = norm_parts(embed[...], current[...])
    scaled = grad_hidden * gain[...][None]
    first_mean = jnp.mean(scaled, axis=-1, keepdims=True)
    second_mean = jnp.mean(scaled * normed, axis=-1, keepdims=True)
    gradient = residual[...] + (scaled - first_mean - normed * second_mean) * inverse
    gradient_ref[...] = gradient
    before = current[...]
    lanes = sums_ref.shape[1]
    sums_ref[...] = jnp.zeros_like(sums_ref)
    for i, terms in enumerate((gradient * gradient, before * gradient, before * before)):
        columns = jnp.sum(terms, axis=0, keepdims=True)
        sums_ref[i : i + 1, :] = sum(
            columns[:, j : j + lanes] for j in range(0, columns.shape[1], lanes)
        )


def finish_body(plane_ref, step_ref, radius_ref, *refs):
    *sum_refs, current, gradient, moved = refs
    sums = jnp.sum(sum(ref[...] for ref in sum_refs), axis=1, keepdims=True)
    grad_square, cross, square = sums[0:1], sums[1:2], sums[2:3]
    plane = plane_ref[0]
    rate = step_ref[plane] / jnp.sqrt(grad_square + norm_epsilon)
    stepped_square = jnp.maximum(square + 2.0 * rate * cross + rate * rate * grad_square, 0.0)
    shrink = jnp.minimum(1.0, radius_ref[plane] / jnp.sqrt(stepped_square + norm_epsilon))
    moved[...] = (current[...] + rate * gradient[...]) * shrink


def plane_plan(patch_embed, perturbation, target, ln_gain, ln_bias, w_qkv, w_out, radius, step_size):
    seq_count, planes = lax.axis_size("seq"), lax.axis_size("head")
    place, plane = lax.axis_index("seq"), lax.axis_index("head")
    chips = seq_count // 2
    chip, core = place // 2, place % 2
    _, part_rows, width = patch_embed.shape
    _, entries, _ = w_qkv.shape
    head_dim = entries // 3
    length = part_rows * seq_count
    half = length // 2
    embed, current, goal = patch_embed[0], perturbation[0], target[0]

    def swap(array, mask):
        return lax.ppermute(array, "seq", [(i, i ^ mask) for i in range(seq_count)])

    def device(chip, core, plane):
        return (chip * 2 + core) * planes + plane

    def hop(array, pairs):
        perm = [
            (device(c, *source), device(c, *dest)) for c in range(chips) for source, dest in pairs
        ]
        return lax.ppermute(array, ("seq", "head"), perm)

    def mirrored(pairs):
        flip = lambda end: (1 - end[0], planes - 1 - end[1])
        return pairs + [(flip(source), flip(dest)) for source, dest in pairs]

    first_hop = mirrored([((0, 1), (0, 0)), ((0, 0), (0, 1)), ((1, 1), (0, 2))])
    later_hops = [
        mirrored([((0, p), (0, p + 1)) for p in range(first, planes - 1)])
        for first in range(1, planes - 1)
    ]

    def chain(array):
        steps = [array, hop(array, first_hop)]
        for pairs in later_hops:
            steps.append(hop(steps[-1], pairs))
        return steps

    distance = jnp.where(core == 0, plane, planes - 1 - plane)
    depth = jnp.maximum(distance - 1, 0)

    shapes = [
        jax.ShapeDtypeStruct((rows, width), bf16)
        for rows in (part_rows, 2 * head_dim, 2 * head_dim)
    ]
    inputs = (embed, current, ln_gain, ln_bias)
    hidden, upper, lower = pl.pallas_call(
        begin_body,
        out_shape=shapes,
        in_specs=[SMEM] * 2 + [HBM] * 6,
        out_specs=[VMEM] * 3,
        scratch_shapes=[pltpu.VMEM(a.shape, a.dtype) for a in inputs]
        + [pltpu.SemaphoreType.DMA((7,))],
        compiler_params=pltpu.CompilerParams(vmem_limit_bytes=VMEM_LIMIT),
        name="bg",
    )(
        chip.reshape(1),
        depth.reshape(1),
        *[pltpu.with_memory_space_constraint(a, pltpu.HBM) for a in (*inputs, w_qkv, w_out)],
    )
    lower_steps = chain(lower)
    upper_steps = chain(upper)

    def gather(array):
        same = [array] + [swap(array, 2 * m) for m in range(1, chips)]
        return same + [swap(part, 1) for part in same]

    def exchange(same, other):
        arrived = swap(other, 1)
        pairs = [jnp.stack([same[m], arrived[m]]) for m in range(chips)]
        return [pairs[0]] + [swap(pairs[m], 2 * m) for m in range(1, chips)]

    hidden_rows = gather(hidden)

    square = length * length
    packed_outs = [((entries, length), bf16), ((entries, width), bf16)]
    attend_outs = [((length, length), bf16), ((head_dim, length), bf16)]
    joined_outs = [((chips, 2 * head_dim, part_rows), bf16)] * 2
    pack_flops = 2 * length * entries * width
    near_packed, near_weight = call(
        functools.partial(packed_body, seq_count, planes - 1),
        packed_outs,
        depth.reshape(1),
        *upper_steps[:-1],
        *lower_steps[:-1],
        *hidden_rows,
        scalars=(0,),
        flops=pack_flops,
    )
    near_kept, near_out = call(
        near_body, attend_outs, near_packed, flops=4 * square * head_dim, exps=square
    )
    far_packed, far_weight, far_kept, far_out, *both_out = call(
        functools.partial(far_body, seq_count, planes - 1),
        packed_outs + attend_outs + joined_outs,
        near_out,
        depth.reshape(1),
        *upper_steps[1:],
        *lower_steps[1:],
        *hidden_rows,
        scalars=(1,),
        flops=pack_flops + 4 * square * head_dim,
        exps=square,
    )
    slots = exchange(*both_out)
    weights = []
    for lowers in (lower_steps[:-1], lower_steps[1:]):
        (own_rows,) = call(
            pick_body, [((head_dim, width), bf16)], depth.reshape(1), *lowers, scalars=(0,)
        )
        weights.append(gather(own_rows))
    weights = [part for pair in zip(*weights) for part in pair]
    *grad_parts, residual = call(
        functools.partial(project_body, len(slots)),
        [((chips, 2 * head_dim, part_rows), bf16)] * 2 + [((part_rows, width), f32)],
        embed,
        current,
        goal,
        *slots,
        *weights,
        flops=4 * part_rows * width * width,
    )
    arrived = exchange(*grad_parts)
    grads, swapped = [], []
    heads = (near_packed, near_kept, near_out), (far_packed, far_kept, far_out)
    for head, (packed, kept, out) in enumerate(heads):
        stay, leave = call(
            functools.partial(backward_body, head),
            [((entries, half), bf16)] * 2,
            packed,
            kept,
            out,
            *arrived,
            flops=8 * length * length * head_dim,
        )
        grads.append(stay)
        swapped.append(swap(leave, 1))
    both = [near_weight, far_weight]
    others = [swap(w, 1) for w in both]
    (partial,) = call(
        partial_body,
        [((half, width), f32)],
        *grads,
        swapped[0],
        *both,
        others[0],
        flops=6 * half * entries * width,
    )
    own, *sent = call(
        hidden_grad_body,
        [((part_rows, width), f32)] + [((part_rows, width), bf16)] * (chips - 1),
        swapped[1],
        others[1],
        partial,
        flops=2 * half * entries * width,
    )
    parts = [swap(part, 2 * (m + 1)) for m, part in enumerate(sent)]
    gradient, sums = call(
        gradient_body,
        [((part_rows, width), f32), ((8, 128), f32)],
        embed,
        current,
        residual,
        ln_gain,
        own,
        *parts,
    )
    sums = sums + swap(sums, 1)
    (moved,) = call(
        finish_body,
        [((part_rows, width), f32)],
        plane.reshape(1),
        step_size,
        radius,
        sums,
        *[swap(sums, 2 * m) for m in range(1, chips)],
        current,
        gradient,
        scalars=(0, 1, 2),
    )
    return moved[None]


def on_device(patch_embed, perturbation, target, ln_gain, ln_bias, w_qkv, w_out, radius, step_size):
    seq_count, planes = lax.axis_size("seq"), lax.axis_size("head")
    own_images, part_rows, _ = patch_embed.shape
    local_heads, entries, _ = w_qkv.shape
    fits = (
        own_images == 1
        and 2 * local_heads == seq_count
        and seq_count == 8
        and planes == 4
        and part_rows % 128 == 0
        and entries % 48 == 0
    )
    plan = plane_plan if fits else general_plan
    return plan(
        patch_embed, perturbation, target, ln_gain, ln_bias, w_qkv, w_out, radius, step_size
    )


def solution(mesh):
    placed = (
        P("head", "seq", None),
        P("head", "seq", None),
        P("head", "seq", None),
        P(),
        P(),
        P("head", None, None),
        P("head", None, None),
        P(),
        P(),
    )
    return jax.shard_map(
        on_device, mesh=mesh, in_specs=placed, out_specs=P("head", "seq", None), check_vma=False
    )
```
